32 devices in a mesh: rows: 4 (over z), cols: 8 (over y, x, core).
Axes of the slice: x: 2, y: 2, z: 4, core: 2. Of those that a mesh axis runs over, the one named last changes fastest.
Arguments:
- left_fine: bfloat16 [128, 1024, 128], P('rows', 'cols'), may hold values from -40 to 40
- right_fine: bfloat16 [128, 1024, 128], P('rows', 'cols'), may hold values from -40 to 40
- left_coarse: bfloat16 [32, 256, 128], P('rows', 'cols'), may hold values from -40 to 40
- right_coarse: bfloat16 [32, 256, 128], P('rows', 'cols'), may hold values from -40 to 40
- candidates: int32 [8, 32, 4], P(None, 'rows'), may hold values from 0 to 7, all different within a row; in each aligned block of 8 rows (0 to 7, 8 to 15, ..., all dimensions but the last counted through in order) at most 8 rows name the same one
- counts: int32 [8, 32], P(None, 'rows'), may hold values from 1 to 4
- query_weight: bfloat16 [128, 128], replicated, may hold values from -1 to 1
- key_weight: bfloat16 [128, 128], replicated, may hold values from -1 to 1
- value_weight: bfloat16 [128, 128], replicated, may hold values from -0.5 to 0.5
- out_weight: bfloat16 [128, 128], replicated, may hold values from -0.5 to 0.5
- norm_gain: float32 [128], replicated, may hold values from 0.5 to 1.5
Outputs:
- fine_features: bfloat16 [128, 1024, 128], P('rows', 'cols')
- coarse_prior: bfloat16 [32, 256, 128], P('rows', 'cols')
The draws below stay inside these ranges and needn't reach their ends.
Inputs may be any that keep to these rules, and one draw needn't show every extreme that they name: `candidates`: each list names 4 different right blocks; entries at k >= counts are not used. For one left block, within the 8 bands of one index of rows (aligned groups of bands), no right block is named more than 8 times, and in some groups one is named exactly 8 times.
All inputs are finite; a program needn't handle non-finite values.
Results may differ from the reference program's by a relative error of at most 0.01.
Values may be sent and summed in bfloat16 or wider, within the bound.
A program may use at most 192 MiB of HBM per device.

```python
import math
import jax
import jax.numpy as jnp
import numpy as np
from jax import lax

FEAT = 128
HEADS = 8
HEAD_DIM = 16
BLOCK = 128
BAND = 4
CANDS = 4
BANDS_DEV = 8
ROWS_FINE = 128
COLS_FINE = 1024
ROWS_COARSE = 32
COLS_COARSE = 256
BANDS = 32
CAP = 8
N_COLS = 8


def background(key, salt, shape):
    values = jnp.clip(jax.random.normal(jax.random.fold_in(key, salt), shape, jnp.float32), -4.0, 4.0)
    return values


def draw_left_fine(key, part):
    values = background(key, 31, (ROWS_FINE, COLS_FINE, FEAT))
    return values.astype(jnp.bfloat16)


def draw_right_fine(key, part):
    values = background(key, 33, (ROWS_FINE, COLS_FINE, FEAT))
    return values.astype(jnp.bfloat16)


def draw_left_coarse(key, part):
    values = background(key, 35, (ROWS_COARSE, COLS_COARSE, FEAT))
    return values.astype(jnp.bfloat16)


def draw_right_coarse(key, part):
    values = background(key, 37, (ROWS_COARSE, COLS_COARSE, FEAT))
    return values.astype(jnp.bfloat16)


def weight_base(key, salt):
    values = jnp.clip(jax.random.normal(jax.random.fold_in(key, salt), (FEAT, FEAT), jnp.float32), -4.0, 4.0)
    return values / jnp.sqrt(jnp.float32(FEAT))


def draw_query_weight(key, part):
    return weight_base(key, 51).astype(jnp.bfloat16)


def draw_key_weight(key, part):
    jitter = weight_base(key, 52)
    values = jitter
    return values.astype(jnp.bfloat16)


def with_ends(entries, stream_key, low, high):
    dims = entries.shape
    place = [jax.random.randint(jax.random.fold_in(stream_key, axis), (), 0, dims[axis]) for axis in range(len(dims))]
    entries = entries.at[tuple(place)].set(low)
    longest = dims.index(max(dims))
    place[longest] = (place[longest] + 1) % dims[longest]
    return entries.at[tuple(place)].set(high)


def shared_out(own_key, own, number, rows, number_of, top, reach, lean):
    order = jax.random.permutation(own_key, number_of)
    packed, common = portions_of(number_of, rows * top, reach, lean, True), portions_of(number_of, rows * top, reach, lean, False)
    places = jnp.arange(number_of)

    def named(tallies, rotation):
        used = int((tallies > 0).sum())
        fixed = max(1, used // 4)
        passed = fixed + (places - fixed + rotation * (used - fixed)) % max(1, number_of - fixed)
        return jnp.zeros((number_of,), jnp.int32).at[order[jnp.where(places < fixed, places, passed)]].set(jnp.asarray(tallies, jnp.int32))

    tallies = jnp.where(number % 4 == 0, named(packed, number // 4), named(common, number - number // 4 - 1))
    mixed = jax.random.permutation(jax.random.fold_in(own, 3), number_of)
    giver, receiver = mixed[0:number_of // 2 * 2:2], mixed[1:number_of // 2 * 2:2]
    room = jnp.minimum(tallies[giver] - 1, reach - tallies[receiver]) // 2
    room = jnp.where((giver == order[0]) | (receiver == order[0]) | (tallies[receiver] == 0), 0, jnp.maximum(room, 0))
    passed = jax.random.randint(jax.random.fold_in(own, 4), (number_of // 2,), 0, 1 << 20) % (room + 1)
    tallies = tallies.at[giver].add(-passed).at[receiver].add(passed)
    labels = jnp.searchsorted(jnp.cumsum(tallies), jnp.arange(rows * top), side="right").astype(jnp.int32)
    table = labels.reshape(top, rows).T
    table = table[jax.random.permutation(jax.random.fold_in(own, 1), rows)]
    rotation = jax.random.randint(jax.random.fold_in(own, 2), (rows, 1), 0, top)
    return jnp.take_along_axis(table, (jnp.arange(top)[None, :] + rotation) % top, axis=1)


def portions_of(amount, total, limit, skew, full):
    weights = [(1 << 20) // math.isqrt(grade ** skew) + 1 for grade in range(1, amount + 1)]
    largest = limit if full else min(limit, max(-(-total // amount), total * weights[0] // sum(weights)))
    least = 1 if total - largest >= amount - 1 else 0
    given, surplus = [largest] + [least] * (amount - 1), total - largest - least * (amount - 1)
    while surplus > 0:
        free = [i for i in range(1, amount) if given[i] < largest] or [i for i in range(1, amount) if given[i] < limit]
        pool, remaining = sum([weights[i] for i in free]), surplus
        for i in free:
            extra = min(limit - given[i], max(1, remaining * weights[i] // pool), surplus)
            given[i] = given[i] + extra
            surplus = surplus - extra
    return np.array(given)


def gaussian(own_key, extent, scale, reach, kind=jnp.bfloat16):
    result = jax.random.normal(own_key, extent, jnp.float32) * scale
    return jnp.minimum(jnp.maximum(result, -reach), reach).astype(kind)


def setup_inputs(seed: int = 0) -> dict:
    seeds = jax.random.split(jax.random.key(seed), 12)
    left_fine = draw_left_fine(jax.random.fold_in(seeds[11], 71), 0)
    right_fine = draw_right_fine(jax.random.fold_in(seeds[11], 71), 0)
    left_coarse = draw_left_coarse(jax.random.fold_in(seeds[11], 71), 0)
    right_coarse = draw_right_coarse(jax.random.fold_in(seeds[11], 71), 0)
    candidates_keys = jax.random.split(jax.random.fold_in(seeds[4], 1), N_COLS * BANDS // BANDS_DEV)
    candidates_turns = jax.random.permutation(jax.random.fold_in(seeds[4], 3), N_COLS * BANDS // BANDS_DEV)
    candidates = jax.vmap(lambda own, number: shared_out(jax.random.fold_in(seeds[4], 2), own, number, BANDS_DEV, N_COLS, CANDS, CAP, 2))(candidates_keys, candidates_turns).reshape((N_COLS, BANDS, CANDS))
    counts = with_ends(jax.random.randint(seeds[5], (N_COLS, BANDS), 1, CANDS + 1), jax.random.fold_in(seeds[5], 1), 1, CANDS).astype(jnp.int32)
    query_weight = draw_query_weight(jax.random.fold_in(seeds[11], 71), 0)
    key_weight = draw_key_weight(jax.random.fold_in(seeds[11], 71), 0)
    value_weight = gaussian(seeds[8], (FEAT, FEAT), FEAT ** -0.5, 0.5)
    out_weight = gaussian(seeds[9], (FEAT, FEAT), FEAT ** -0.5, 0.5)
    norm_gain = jnp.clip(1.0 + 0.1 * jax.random.normal(seeds[10], (FEAT,), jnp.float32), 0.5, 1.5)
    return {"left_fine": left_fine, "right_fine": right_fine, "left_coarse": left_coarse, "right_coarse": right_coarse, "candidates": candidates, "counts": counts, "query_weight": query_weight, "key_weight": key_weight, "value_weight": value_weight, "out_weight": out_weight, "norm_gain": norm_gain}


EPSILON = 1e-05

def layer_norm(values, norm_gain):
    average = lax.optimization_barrier(jnp.mean(values, axis=-1, keepdims=True))
    centred = values - average
    spread = lax.optimization_barrier(jnp.mean(centred * centred, axis=-1, keepdims=True))
    return centred * lax.rsqrt(spread + EPSILON) * norm_gain

def project(values, weight):
    flat_rows = values.reshape(-1, values.shape[-1])
    product = jnp.dot(flat_rows, weight, preferred_element_type=jnp.float32)
    return product.astype(jnp.bfloat16).reshape(values.shape[:-1] + (weight.shape[1],))

def split_heads(values):
    return values.reshape(values.shape[:-1] + (HEADS, HEAD_DIM)).astype(jnp.float32)

def blend(values, axis_pos, before_rows, after_rows):
    stacked = jnp.stack([0.375 * before_rows + 0.625 * values, 0.125 * before_rows + 0.875 * values, 0.875 * values + 0.125 * after_rows, 0.625 * values + 0.375 * after_rows], axis=axis_pos + 1)
    new_shape = values.shape[:axis_pos] + (4 * values.shape[axis_pos],) + values.shape[axis_pos + 1:]
    return stacked.reshape(new_shape)

def reference(left_fine, right_fine, left_coarse, right_coarse, candidates, counts, query_weight, key_weight, value_weight, out_weight, norm_gain):
    scale_factor = 1.0 / math.sqrt(HEAD_DIM)
    coarse_query = project(left_coarse, query_weight)
    coarse_key = project(right_coarse, key_weight)
    coarse_value = project(right_coarse, value_weight)

    def coarse_row(inputs):
        row_query, row_key, row_value = inputs
        scores = jnp.einsum('qhd,khd->hqk', split_heads(row_query), split_heads(row_key)) * scale_factor
        weights = jax.nn.softmax(scores, axis=-1).astype(jnp.bfloat16)
        mixture = jnp.einsum('hqk,khd->qhd', weights.astype(jnp.float32), split_heads(row_value))
        return mixture.astype(jnp.bfloat16).reshape(row_query.shape)
    coarse_attn = lax.map(coarse_row, (coarse_query, coarse_key, coarse_value))
    coarse_mix = jnp.dot(coarse_attn.reshape(-1, FEAT), out_weight, preferred_element_type=jnp.float32)
    coarse_mix = coarse_mix.reshape(left_coarse.shape)
    coarse_prior = layer_norm(left_coarse.astype(jnp.float32) + coarse_mix, norm_gain).astype(jnp.bfloat16)
    prior_float = coarse_prior.astype(jnp.float32)

    def fine_band(inputs):
        band_index, left_rows, right_rows, band_cands, band_counts = inputs
        middle_row = lax.dynamic_index_in_dim(prior_float, band_index, 0, keepdims=True)
        lower_row = lax.dynamic_index_in_dim(prior_float, jnp.maximum(band_index - 1, 0), 0, keepdims=True)
        upper_row = lax.dynamic_index_in_dim(prior_float, jnp.minimum(band_index + 1, ROWS_COARSE - 1), 0, keepdims=True)
        row_up = blend(middle_row, 0, lower_row, upper_row)
        left_cols = jnp.concatenate([row_up[:, :1], row_up[:, :-1]], axis=1)
        right_cols = jnp.concatenate([row_up[:, 1:], row_up[:, -1:]], axis=1)
        upsampled = blend(row_up, 1, left_cols, right_cols)
        query_in = (left_rows.astype(jnp.float32) + upsampled).astype(jnp.bfloat16)
        queries = project(query_in, query_weight).reshape(BAND, N_COLS, BLOCK, FEAT)
        keys_band = project(right_rows, key_weight).reshape(BAND, N_COLS, BLOCK, FEAT)
        values_band = project(right_rows, value_weight).reshape(BAND, N_COLS, BLOCK, FEAT)
        picked_keys = keys_band[:, band_cands]
        picked_values = values_band[:, band_cands]
        scores = jnp.einsum('rbqhd,rbckhd->brhqck', split_heads(queries), split_heads(picked_keys)) * scale_factor
        usable = jnp.arange(CANDS, dtype=jnp.int32)[None, :] < band_counts[:, None]
        scores = jnp.where(usable[:, None, None, None, :, None], scores, -1e+30)
        flat_scores = scores.reshape(scores.shape[:4] + (CANDS * BLOCK,))
        weights = jax.nn.softmax(flat_scores, axis=-1).astype(jnp.bfloat16).reshape(scores.shape)
        mixture = jnp.einsum('brhqck,rbckhd->rbqhd', weights.astype(jnp.float32), split_heads(picked_values))
        mixture = mixture.astype(jnp.bfloat16).reshape(BAND * COLS_FINE, FEAT)
        fine_mix = jnp.dot(mixture, out_weight, preferred_element_type=jnp.float32).reshape(BAND, COLS_FINE, FEAT)
        return layer_norm(query_in.astype(jnp.float32) + fine_mix, norm_gain).astype(jnp.bfloat16)
    band_ids = jnp.arange(BANDS, dtype=jnp.int32)
    fine_out = lax.map(fine_band, (band_ids, left_fine.reshape(BANDS, BAND, COLS_FINE, FEAT), right_fine.reshape(BANDS, BAND, COLS_FINE, FEAT), jnp.transpose(candidates, (1, 0, 2)), jnp.transpose(counts, (1, 0))))
    return (fine_out.reshape(ROWS_FINE, COLS_FINE, FEAT), coarse_prior)
```

```python
import functools
import math

import jax
import jax.numpy as jnp
import numpy as np
from jax import lax
from jax.experimental import pallas as pl
from jax.experimental.pallas import tpu as pltpu
from jax.sharding import PartitionSpec as P

HEADS = 8
HEAD_DIM = 16
BLOCK = 128
BAND = 4
EPSILON = 1e-05
PAIRS = HEADS // 2
EDGE = 16
LEAD = 3
AHEAD = 3
SLOTS = AHEAD + 1
STEPS = BAND * PAIRS
MESH = pl.DeviceIdType.MESH
KEY_SCALE = math.log2(math.e) / math.sqrt(HEAD_DIM)
BF16 = jnp.bfloat16
F32 = jnp.float32


def nt(a, b):
    return lax.dot_general(a, b, (((1,), (1,)), ((), ())), preferred_element_type=F32)


def tn(a, b):
    return lax.dot_general(a, b, (((0,), (0,)), ((), ())), preferred_element_type=F32)


def nn(a, b):
    return jnp.dot(a, b, preferred_element_type=F32)


def layer_norm(values, norm_gain):
    average = jnp.mean(values, axis=-1, keepdims=True)
    centred = values - average
    spread = jnp.mean(centred * centred, axis=-1, keepdims=True)
    return centred * lax.rsqrt(spread + EPSILON) * norm_gain


def upsample_matrix(cols):
    taps = np.array(
        [[0.375, 0.625, 0.0], [0.125, 0.875, 0.0], [0.0, 0.875, 0.125], [0.0, 0.625, 0.375]]
    )
    pitch = cols + 2 * EDGE
    out = np.zeros((BAND, cols, 4, 3, pitch), np.float32)
    for c in range(cols):
        for t in range(4):
            for d in range(3):
                out[:, c, t, :, c + d + EDGE - 1] = taps[:, :] * taps[t, d]
    return out.reshape(BAND * cols * 4, 3 * pitch)


def flipped(index, bit):
    return index + bit - 2 * bit * ((index // bit) % 2)


def gather_hops(n, me):
    if n != 8:
        return [(me, (me + j) % n, None) for j in range(1, n)]
    a, b, c = flipped(me, 1), flipped(me, 2), flipped(me, 4)
    d = flipped(b, 4)
    odd = me % 2
    relay_block = b + odd * (c - b)
    relay_target = c + odd * (b - c)
    return [
        (me, b, None),
        (me, c, None),
        (me, a, None),
        (relay_block, relay_target, (0, 1)),
        (b, a, (0,)),
        (c, a, (1,)),
        (d, a, (3,)),
    ]


def column_top(scores):
    rows, cols = scores.shape
    tile = jnp.max(scores.reshape(rows // 8, 8, cols), axis=0)
    return jnp.broadcast_to(jnp.max(tile, axis=0, keepdims=True), (8, cols))


def shifted_weights(scores, top):
    rows, cols = scores.shape
    shifted = scores.reshape(rows // 8, 8, cols) - top[None]
    return jnp.exp2(shifted.reshape(rows, cols).astype(BF16))


def kernel(
    list_ref,
    count_ref,
    left_hbm,
    right_ref,
    left_coarse_ref,
    right_coarse_ref,
    up_ref,
    wq_ref,
    wk_ref,
    wv_ref,
    wo_ref,
    gain_ref,
    fold_ref,
    fine_hbm,
    prior_ref,
    *scratch,
    n,
    row_devices,
    bands,
):
    bands_ref = scratch[:bands]
    (
        left_ref,
        fine_ref,
        coarse_ref,
        ext_ref,
        wqt_ref,
        wvt_ref,
        coarse_keys,
        coarse_values,
        coarse_query,
        coarse_scores,
        coarse_top,
        picked_ref,
        query_in_ref,
        query_ref,
        keys_ref,
        values_ref,
        spread_ref,
        scores_ref,
        top_ref,
        mix_ref,
        coarse_send,
        coarse_recv,
        edge_send,
        edge_recv,
        fine_send,
        fine_recv,
        own_sem,
        left_sem,
        out_sem,
    ) = scratch[bands:]
    me = lax.axis_index("cols")
    row = lax.axis_index("rows")
    coarse_rows, coarse_cols, feat = left_coarse_ref.shape
    length = list_ref.shape[1]
    hops = gather_hops(n, me)

    inside = {
        -1: (row > 0, me > 0),
        0: (True, True),
        1: (row < row_devices - 1, me < n - 1),
    }
    sides = [(dy, dx) for dy in (-1, 0, 1) for dx in (-1, 0, 1) if dy or dx]

    def reach(dy, dx):
        return jnp.logical_and(inside[dy][0], inside[dx][1])

    barrier = pltpu.get_barrier_semaphore()
    for j in range(1, n):
        pl.semaphore_signal(
            barrier, inc=1, device_id={"cols": (me + j) % n}, device_id_type=MESH
        )
    expected = n - 1
    for dy, dx in sides:
        if dy:
            there = reach(dy, dx)

            @pl.when(there)
            def _(dy=dy, dx=dx):
                pl.semaphore_signal(
                    barrier,
                    inc=1,
                    device_id={"rows": row + dy, "cols": me + dx},
                    device_id_type=MESH,
                )

            expected = expected + there.astype(jnp.int32)

    def left_copy():
        return pltpu.make_async_copy(left_hbm, left_ref, left_sem.at[0])

    def own_copy(g):
        return pltpu.make_async_copy(
            right_ref.at[pl.ds(g * BAND, BAND)], bands_ref[g].at[me], own_sem.at[g]
        )

    left_copy().start()
    for g in range(bands):
        own_copy(g).start()
    pl.semaphore_wait(barrier, expected)

    def coarse_copy(hop):
        block, target, after = hops[hop]
        return pltpu.make_async_remote_copy(
            src_ref=right_coarse_ref if after is None else coarse_ref.at[block],
            dst_ref=coarse_ref.at[block],
            send_sem=coarse_send.at[hop],
            recv_sem=coarse_recv.at[hop],
            device_id={"cols": target},
            device_id_type=MESH,
        )

    def fine_copy(g, hop):
        block, target, after = hops[hop]
        if after is None:
            source = right_ref.at[pl.ds(g * BAND, BAND)]
        else:
            source = bands_ref[g].at[block]
        return pltpu.make_async_remote_copy(
            src_ref=source,
            dst_ref=bands_ref[g].at[block],
            send_sem=fine_send.at[g, hop],
            recv_sem=fine_recv.at[g, hop],
            device_id={"cols": target},
            device_id_type=MESH,
        )

    levels = []
    for hop in hops:
        levels.append(0 if hop[2] is None else 1 + max(levels[i] for i in hop[2]))
    depth = max(levels)
    ends = [i for i in range(len(hops)) if all(i not in (hop[2] or ()) for hop in hops)]
    taken = set()

    def take(copy, kind, hop):
        if (kind, hop) not in taken:
            taken.add((kind, hop))
            copy(hop).wait_recv()

    def send(copy, kind, level):
        for hop in range(len(hops)):
            if levels[hop] == level:
                for needed in hops[hop][2] or ():
                    take(copy, kind, needed)
                copy(hop).start()

    def send_fine(g, level):
        if 0 <= g < bands:
            send(functools.partial(fine_copy, g), g, level)

    for level in range(1):
        send(coarse_copy, "coarse", level)
    send_fine(0, 0)
    coarse_ref[me] = right_coarse_ref[...]
    wqt_ref[...] = wq_ref[...].T
    wvt_ref[...] = wv_ref[...].T
    spread_ref[...] = jnp.zeros_like(spread_ref)
    left_all = left_coarse_ref[...].reshape(coarse_rows * coarse_cols, feat)
    coarse_query[...] = nn(left_all, wq_ref[...]).astype(BF16)
    for level in range(1, depth + 1):
        send(coarse_copy, "coarse", level)
    for g in range(1, LEAD):
        send_fine(g, 0)
    for hop in range(len(hops)):
        take(coarse_copy, "coarse", hop)

    wide = HEADS * coarse_cols
    many = n * coarse_cols
    own_head = (
        lax.broadcasted_iota(jnp.int32, (wide, feat), 0) // coarse_cols
        == lax.broadcasted_iota(jnp.int32, (wide, feat), 1) // HEAD_DIM
    )
    diagonal = (
        lax.broadcasted_iota(jnp.int32, (feat, wide), 0) // HEAD_DIM
        == lax.broadcasted_iota(jnp.int32, (feat, wide), 1) // coarse_cols
    )

    def coarse_project(r):
        right = coarse_ref[:, r].reshape(many, feat)
        coarse_keys[r] = (nn(right, wk_ref[...]) * KEY_SCALE).astype(BF16)
        coarse_values[r] = nt(wvt_ref[...], right).astype(BF16)

    def coarse_score(r):
        query = coarse_query[r * coarse_cols : (r + 1) * coarse_cols]
        query = jnp.where(own_head, jnp.concatenate([query] * HEADS, axis=0), 0).astype(BF16)
        scores = nt(coarse_keys[r], query)
        coarse_scores[r] = scores
        coarse_top[r] = column_top(scores)

    def coarse_finish(r):
        weights = shifted_weights(coarse_scores[r], coarse_top[r])
        ones = jnp.ones((EDGE, many), BF16)
        mixed = nn(jnp.concatenate([coarse_values[r], ones], axis=0), weights)
        mixed = mixed[:feat] * (1.0 / mixed[feat : feat + 1])
        mixed = jnp.where(diagonal, mixed, 0.0).astype(BF16)
        folded = nt(fold_ref[...], mixed).astype(BF16)
        out = left_coarse_ref[r].astype(F32) + nn(folded, wo_ref[...])
        out = layer_norm(out, gain_ref[...]).astype(BF16)
        ext_ref[r + 1, EDGE : EDGE + coarse_cols] = out
        prior_ref[r] = out

    for r in range(coarse_rows + 2):
        if r < coarse_rows:
            coarse_project(r)
        if 1 <= r <= coarse_rows:
            coarse_score(r - 1)
        if r >= 2:
            coarse_finish(r - 2)

    def part(d, size, away):
        span = coarse_rows if size is None else coarse_cols
        base = 1 if size is None else EDGE
        pad = 1 if size is None else EDGE
        if d == 0:
            return pl.ds(base, span)
        if away:
            return pl.ds(base if d < 0 else base + span - pad, pad)
        return pl.ds(base + span if d < 0 else base - pad, pad)

    def edge_copy(i):
        dy, dx = sides[i]
        return pltpu.make_async_remote_copy(
            src_ref=ext_ref.at[part(dy, None, True), part(dx, EDGE, True)],
            dst_ref=ext_ref.at[part(dy, None, False), part(dx, EDGE, False)],
            send_sem=edge_send.at[i],
            recv_sem=edge_recv.at[i],
            device_id={"rows": row + dy, "cols": me + dx},
            device_id_type=MESH,
        )

    for i, (dy, dx) in enumerate(sides):

        @pl.when(reach(dy, dx))
        def _(i=i):
            edge_copy(i).start()

    send_fine(0, 1)
    send_fine(LEAD, 0)

    for i, (dy, dx) in enumerate(sides):

        @pl.when(reach(dy, dx))
        def _(i=i):
            edge_copy(i).wait_send()

        @pl.when(reach(-dy, -dx))
        def _(i=i):
            edge_copy(i).wait_recv()

    last = EDGE + coarse_cols

    @pl.when(me == 0)
    def _():
        ext_ref[:, :EDGE] = jnp.broadcast_to(
            ext_ref[:, EDGE : EDGE + 1], (coarse_rows + 2, EDGE, feat)
        )

    @pl.when(me == n - 1)
    def _():
        ext_ref[:, last:] = jnp.broadcast_to(
            ext_ref[:, last - 1 : last], (coarse_rows + 2, EDGE, feat)
        )

    @pl.when(row == 0)
    def _():
        ext_ref[0] = ext_ref[1]

    @pl.when(row == row_devices - 1)
    def _():
        ext_ref[coarse_rows + 1] = ext_ref[coarse_rows]

    left_copy().wait()
    for level in range(2, depth + 1):
        send_fine(0, level)

    def branches(g, action):
        for fixed in range(bands):
            pl.when(g == fixed)(functools.partial(action, fixed))

    def enter(g):
        send_fine(g + 1, 1)
        send_fine(g + 1 + LEAD, 0)
        own_copy(g).wait()
        for hop in ends:
            take(functools.partial(fine_copy, g), g, hop)
        used = count_ref[me, g]
        first = list_ref[me, 0, g]
        for k in range(length):
            pick = first if k == 0 else jnp.where(k < used, list_ref[me, k, g], first)
            picked_ref[:, k * BLOCK : (k + 1) * BLOCK] = bands_ref[g][pick]

    def middle(g):
        for level in range(2, depth + 1):
            send_fine(g + 1, level)

    def band_step(g, carry):
        branches(g, enter)
        used = count_ref[me, g]
        lanes = lax.broadcasted_iota(jnp.int32, (1, length * BLOCK), 1)
        live = jnp.where(lanes < used * BLOCK, 1.0, 0.0).astype(BF16)
        ones = jnp.broadcast_to(live, (HEAD_DIM, length * BLOCK))

        coarse = jnp.concatenate([ext_ref[g + i] for i in range(3)], axis=0)
        up = nn(up_ref[...], coarse)
        left = left_ref[pl.ds(g * BAND, BAND)].reshape(up.shape)
        query_in = (left.astype(F32) + up).astype(BF16)
        query_in_ref[...] = query_in
        query_ref[...] = nt(wqt_ref[...], query_in).astype(BF16)

        def prepare(r):
            right = picked_ref[r]
            keys_ref[r] = (nn(right, wk_ref[...]) * KEY_SCALE).astype(BF16)
            values_ref[r] = nt(wvt_ref[...], right).astype(BF16) * live
            for h in range(HEADS):
                rows = slice(h * HEAD_DIM, (h + 1) * HEAD_DIM)
                spread_ref[r, rows, h * BLOCK : (h + 1) * BLOCK] = query_ref[
                    rows, r * BLOCK : (r + 1) * BLOCK
                ]

        def score(i):
            r, pair = divmod(i, PAIRS)
            top = None
            for k in range(length):
                keys = keys_ref[r, k * BLOCK : (k + 1) * BLOCK]
                part = nn(keys, spread_ref[r, :, pair * 2 * BLOCK : (pair + 1) * 2 * BLOCK])
                scores_ref[i % SLOTS, k * BLOCK : (k + 1) * BLOCK] = part
                tile = jnp.max(part.reshape(BLOCK // 8, 8, 2 * BLOCK), axis=0)
                top = tile if top is None else jnp.maximum(top, tile)
            top_ref[i % SLOTS] = jnp.broadcast_to(
                jnp.max(top, axis=0, keepdims=True), (8, 2 * BLOCK)
            )

        def process(i):
            r, pair = divmod(i, PAIRS)
            weights = shifted_weights(scores_ref[i % SLOTS], top_ref[i % SLOTS])
            rows = slice(pair * 2 * HEAD_DIM, (pair + 1) * 2 * HEAD_DIM)
            mixed = nn(jnp.concatenate([values_ref[r, rows], ones], axis=0), weights)
            inverse = 1.0 / mixed[2 * HEAD_DIM : 2 * HEAD_DIM + 1]
            here = slice(r * BLOCK, (r + 1) * BLOCK)
            start = pair * 2 * HEAD_DIM
            mix_ref[start : start + HEAD_DIM, here] = (
                mixed[:HEAD_DIM, :BLOCK] * inverse[:, :BLOCK]
            ).astype(BF16)
            mix_ref[start + HEAD_DIM : start + 2 * HEAD_DIM, here] = (
                mixed[HEAD_DIM : 2 * HEAD_DIM, BLOCK:] * inverse[:, BLOCK:]
            ).astype(BF16)

        prepare(0)
        for i in range(AHEAD):
            score(i)
        for i in range(STEPS):
            if i % PAIRS == 0 and i // PAIRS + 1 < BAND:
                prepare(i // PAIRS + 1)
            if i + AHEAD < STEPS:
                score(i + AHEAD)
            process(i)
            if i == STEPS // 2 - 1:
                branches(g, middle)

        product = tn(mix_ref[...], wo_ref[...])
        out = layer_norm(query_in_ref[...].astype(F32) + product, gain_ref[...]).astype(BF16)
        here = pl.ds(g * BAND, BAND)
        fine_ref[here] = out.reshape(BAND, BLOCK, feat)
        pltpu.make_async_copy(fine_ref.at[here], fine_hbm.at[here], out_sem.at[g]).start()
        return carry

    lax.fori_loop(0, bands, band_step, 0)

    for hop in range(len(hops)):
        coarse_copy(hop).wait_send()
    for g in range(bands):
        for hop in range(len(hops)):
            fine_copy(g, hop).wait_send()
        here = pl.ds(g * BAND, BAND)
        pltpu.make_async_copy(fine_ref.at[here], fine_hbm.at[here], out_sem.at[g]).wait()


def body(
    left_fine,
    right_fine,
    left_coarse,
    right_coarse,
    candidates,
    counts,
    query_weight,
    key_weight,
    value_weight,
    out_weight,
    norm_gain,
):
    n = lax.axis_size("cols")
    rows, cols, feat = left_fine.shape
    bands = rows // BAND
    coarse_rows, coarse_cols, _ = left_coarse.shape
    length = candidates.shape[2]
    up = upsample_matrix(coarse_cols)
    fold = np.tile(np.eye(coarse_cols, dtype=np.float32), (1, HEADS))
    hop_count = len(gather_hops(n, 0))
    many = n * coarse_cols
    wide = HEADS * coarse_cols
    vmem = pl.BlockSpec(memory_space=pltpu.VMEM)
    smem = pl.BlockSpec(memory_space=pltpu.SMEM)
    hbm = pl.BlockSpec(memory_space=pl.ANY)
    return pl.pallas_call(
        functools.partial(kernel, n=n, row_devices=lax.axis_size("rows"), bands=bands),
        out_shape=(
            jax.ShapeDtypeStruct(left_fine.shape, BF16),
            jax.ShapeDtypeStruct(left_coarse.shape, BF16),
        ),
        in_specs=[smem, smem, hbm, hbm] + [vmem] * 9,
        out_specs=(hbm, vmem),
        scratch_shapes=[pltpu.VMEM((n, BAND, cols, feat), BF16) for _ in range(bands)]
        + [
            pltpu.VMEM(left_fine.shape, BF16),
            pltpu.VMEM(left_fine.shape, BF16),
            pltpu.VMEM((n,) + right_coarse.shape, BF16),
            pltpu.VMEM((coarse_rows + 2, coarse_cols + 2 * EDGE, feat), BF16),
            pltpu.VMEM((feat, feat), BF16),
            pltpu.VMEM((feat, feat), BF16),
            pltpu.VMEM((coarse_rows, many, feat), BF16),
            pltpu.VMEM((coarse_rows, feat, many), BF16),
            pltpu.VMEM((coarse_rows * coarse_cols, feat), BF16),
            pltpu.VMEM((coarse_rows, many, wide), F32),
            pltpu.VMEM((coarse_rows, 8, wide), F32),
            pltpu.VMEM((BAND, length * BLOCK, feat), BF16),
            pltpu.VMEM((BAND * BLOCK, feat), BF16),
            pltpu.VMEM((feat, BAND * BLOCK), BF16),
            pltpu.VMEM((BAND, length * BLOCK, feat), BF16),
            pltpu.VMEM((BAND, feat, length * BLOCK), BF16),
            pltpu.VMEM((BAND, feat, HEADS * BLOCK), BF16),
            pltpu.VMEM((SLOTS, length * BLOCK, 2 * BLOCK), F32),
            pltpu.VMEM((SLOTS, 8, 2 * BLOCK), F32),
            pltpu.VMEM((feat, BAND * BLOCK), BF16),
            pltpu.SemaphoreType.DMA((hop_count,)),
            pltpu.SemaphoreType.DMA((hop_count,)),
            pltpu.SemaphoreType.DMA((8,)),
            pltpu.SemaphoreType.DMA((8,)),
            pltpu.SemaphoreType.DMA((bands, hop_count)),
            pltpu.SemaphoreType.DMA((bands, hop_count)),
            pltpu.SemaphoreType.DMA((bands,)),
            pltpu.SemaphoreType.DMA((1,)),
            pltpu.SemaphoreType.DMA((bands,)),
        ],
        compiler_params=pltpu.CompilerParams(
            collective_id=0, has_side_effects=True, vmem_limit_bytes=60 * 1024 * 1024
        ),
        name="stereo",
    )(
        jnp.transpose(candidates, (0, 2, 1)),
        counts,
        left_fine,
        right_fine,
        left_coarse,
        right_coarse,
        jnp.asarray(up, BF16),
        query_weight,
        key_weight,
        value_weight,
        out_weight,
        norm_gain.reshape(1, -1),
        jnp.asarray(fold, BF16),
    )


def solution(mesh):
    return jax.shard_map(
        body,
        mesh=mesh,
        in_specs=(
            P("rows", "cols", None),
            P("rows", "cols", None),
            P("rows", "cols", None),
            P("rows", "cols", None),
            P(None, "rows", None),
            P(None, "rows"),
            P(),
            P(),
            P(),
            P(),
            P(),
        ),
        out_specs=(P("rows", "cols", None), P("rows", "cols", None)),
        check_vma=False,
    )
```

```python
import functools
import math

import jax
import jax.numpy as jnp
import numpy as np
from jax import lax
from jax.experimental import pallas as pl
from jax.experimental.pallas import tpu as pltpu
from jax.sharding import PartitionSpec as P

HEADS = 8
HEAD_DIM = 16
BLOCK = 128
BAND = 4
EPSILON = 1e-05
PAIRS = HEADS // 2
EDGE = 16
LEAD = 3
EARLY = 2
AHEAD = 3
SLOTS = AHEAD + 1
STEPS = BAND * PAIRS
RELAY_STEP = 3
FORWARD_STEP = 9
MESH = pl.DeviceIdType.MESH
KEY_SCALE = math.log2(math.e) / math.sqrt(HEAD_DIM)
BF16 = jnp.bfloat16
F32 = jnp.float32


def nt(a, b):
    return lax.dot_general(a, b, (((1,), (1,)), ((), ())), preferred_element_type=F32)


def tn(a, b):
    return lax.dot_general(a, b, (((0,), (0,)), ((), ())), preferred_element_type=F32)


def nn(a, b):
    return jnp.dot(a, b, preferred_element_type=F32)


def layer_norm(values, norm_gain):
    average = jnp.mean(values, axis=-1, keepdims=True)
    centred = values - average
    spread = jnp.mean(centred * centred, axis=-1, keepdims=True)
    return centred * lax.rsqrt(spread + EPSILON) * norm_gain


def upsample_matrix(cols):
    taps = np.array(
        [[0.375, 0.625, 0.0], [0.125, 0.875, 0.0], [0.0, 0.875, 0.125], [0.0, 0.625, 0.375]]
    )
    pitch = cols + 2 * EDGE
    out = np.zeros((BAND, cols, 4, 3, pitch), np.float32)
    for c in range(cols):
        for t in range(4):
            for d in range(3):
                out[:, c, t, :, c + d + EDGE - 1] = taps[:, :] * taps[t, d]
    return out.reshape(BAND * cols * 4, 3 * pitch)


def flipped(index, bit):
    return index + bit - 2 * bit * ((index // bit) % 2)


def gather_hops(n, me):
    if n != 8:
        return [(me, (me + j) % n, None) for j in range(1, n)]
    a, b, c = flipped(me, 1), flipped(me, 2), flipped(me, 4)
    d = flipped(b, 4)
    odd = me % 2
    relay_block = b + odd * (c - b)
    relay_target = c + odd * (b - c)
    return [
        (me, b, None),
        (me, c, None),
        (me, a, None),
        (relay_block, relay_target, (0, 1)),
        (b, a, (0,)),
        (c, a, (1,)),
        (d, a, (3,)),
    ]


def coarse_hops(n, me):
    if n != 8:
        return [(me, (me + j) % n, None) for j in range(1, n)]
    a, b, c = flipped(me, 1), flipped(me, 2), flipped(me, 4)
    d = flipped(b, 4)
    return [
        (me, b, None),
        (me, c, None),
        (me, d, None),
        (me, a, None),
        (b, a, (0,)),
        (c, a, (1,)),
        (d, a, (2,)),
    ]


def hop_levels(hops):
    levels = []
    for hop in hops:
        levels.append(0 if hop[2] is None else 1 + max(levels[i] for i in hop[2]))
    return levels


def final_hops(hops):
    used = {i for hop in hops for i in hop[2] or ()}
    return [i for i in range(len(hops)) if i not in used]


def column_top(scores):
    rows, cols = scores.shape
    tile = jnp.max(scores.reshape(rows // 8, 8, cols), axis=0)
    return jnp.broadcast_to(jnp.max(tile, axis=0, keepdims=True), (8, cols))


def shifted_weights(scores, top):
    rows, cols = scores.shape
    shifted = scores.reshape(rows // 8, 8, cols) - top[None]
    return jnp.exp2(shifted.reshape(rows, cols).astype(BF16))


def kernel(
    list_ref,
    count_ref,
    left_hbm,
    right_ref,
    left_coarse_ref,
    right_coarse_ref,
    up_ref,
    wq_ref,
    wk_ref,
    wv_ref,
    wo_ref,
    gain_ref,
    fold_ref,
    fine_hbm,
    prior_ref,
    *scratch,
    n,
    row_devices,
    bands,
):
    bands_ref = scratch[:bands]
    (
        left_ref,
        fine_ref,
        coarse_ref,
        ext_ref,
        wqt_ref,
        wvt_ref,
        coarse_keys,
        coarse_values,
        coarse_query,
        coarse_scores,
        coarse_top,
        picked_ref,
        query_in_ref,
        query_ref,
        keys_ref,
        values_ref,
        spread_ref,
        scores_ref,
        top_ref,
        mix_ref,
        coarse_send,
        coarse_recv,
        edge_send,
        edge_recv,
        fine_send,
        fine_recv,
        own_sem,
        left_sem,
        out_sem,
    ) = scratch[bands:]
    me = lax.axis_index("cols")
    row = lax.axis_index("rows")
    coarse_rows, coarse_cols, feat = left_coarse_ref.shape
    length = list_ref.shape[1]
    fine_hops = gather_hops(n, me)
    start_hops = coarse_hops(n, me)

    inside = {
        -1: (row > 0, me > 0),
        0: (True, True),
        1: (row < row_devices - 1, me < n - 1),
    }
    sides = [(dy, dx) for dy in (-1, 0, 1) for dx in (-1, 0, 1) if dy or dx]

    def reach(dy, dx):
        return jnp.logical_and(inside[dy][0], inside[dx][1])

    barrier = pltpu.get_barrier_semaphore()
    for j in range(1, n):
        pl.semaphore_signal(
            barrier, inc=1, device_id={"cols": (me + j) % n}, device_id_type=MESH
        )
    expected = n - 1
    for dy, dx in sides:
        if dy:
            there = reach(dy, dx)

            @pl.when(there)
            def _(dy=dy, dx=dx):
                pl.semaphore_signal(
                    barrier,
                    inc=1,
                    device_id={"rows": row + dy, "cols": me + dx},
                    device_id_type=MESH,
                )

            expected = expected + there.astype(jnp.int32)

    def left_copy():
        return pltpu.make_async_copy(left_hbm, left_ref, left_sem.at[0])

    def own_copy(g):
        return pltpu.make_async_copy(
            right_ref.at[pl.ds(g * BAND, BAND)], bands_ref[g].at[me], own_sem.at[g]
        )

    left_copy().start()
    for g in range(bands):
        own_copy(g).start()
    pl.semaphore_wait(barrier, expected)

    def coarse_copy(hop):
        block, target, after = start_hops[hop]
        return pltpu.make_async_remote_copy(
            src_ref=right_coarse_ref if after is None else coarse_ref.at[block],
            dst_ref=coarse_ref.at[block],
            send_sem=coarse_send.at[hop],
            recv_sem=coarse_recv.at[hop],
            device_id={"cols": target},
            device_id_type=MESH,
        )

    def fine_copy(g, hop):
        block, target, after = fine_hops[hop]
        if after is None:
            source = right_ref.at[pl.ds(g * BAND, BAND)]
        else:
            source = bands_ref[g].at[block]
        return pltpu.make_async_remote_copy(
            src_ref=source,
            dst_ref=bands_ref[g].at[block],
            send_sem=fine_send.at[g, hop],
            recv_sem=fine_recv.at[g, hop],
            device_id={"cols": target},
            device_id_type=MESH,
        )

    def send(copy, hops, level):
        levels = hop_levels(hops)
        ready = set()
        for hop in range(len(hops)):
            if levels[hop] == level:
                for needed in hops[hop][2] or ():
                    if needed not in ready and levels[needed] == level - 1:
                        ready.add(needed)
                        copy(needed).wait_recv()
                copy(hop).start()

    def send_fine(g, level):
        if 0 <= g < bands:
            send(functools.partial(fine_copy, g), fine_hops, level)

    fine_depth = max(hop_levels(fine_hops))
    coarse_depth = max(hop_levels(start_hops))

    send(coarse_copy, start_hops, 0)
    for g in range(EARLY):
        send_fine(g, 0)
    coarse_ref[me] = right_coarse_ref[...]
    wqt_ref[...] = wq_ref[...].T
    wvt_ref[...] = wv_ref[...].T
    spread_ref[...] = jnp.zeros_like(spread_ref)
    mix_ref[...] = jnp.zeros_like(mix_ref)
    left_all = left_coarse_ref[...].reshape(coarse_rows * coarse_cols, feat)
    coarse_query[...] = nn(left_all, wq_ref[...]).astype(BF16)
    for level in range(1, coarse_depth + 1):
        send(coarse_copy, start_hops, level)
    for g in range(EARLY, LEAD):
        send_fine(g, 0)
    for hop in final_hops(start_hops):
        coarse_copy(hop).wait_recv()

    def relay(g):
        send_fine(g, 1)
        send_fine(g + LEAD, 0)

    def forward(g):
        for level in range(2, fine_depth + 1):
            send_fine(g, level)

    wide = HEADS * coarse_cols
    many = n * coarse_cols
    own_head = (
        lax.broadcasted_iota(jnp.int32, (wide, feat), 0) // coarse_cols
        == lax.broadcasted_iota(jnp.int32, (wide, feat), 1) // HEAD_DIM
    )
    diagonal = (
        lax.broadcasted_iota(jnp.int32, (feat, wide), 0) // HEAD_DIM
        == lax.broadcasted_iota(jnp.int32, (feat, wide), 1) // coarse_cols
    )

    def coarse_project(r):
        right = coarse_ref[:, r].reshape(many, feat)
        coarse_keys[r] = (nn(right, wk_ref[...]) * KEY_SCALE).astype(BF16)
        coarse_values[r] = nt(wvt_ref[...], right).astype(BF16)

    def coarse_score(r):
        query = coarse_query[r * coarse_cols : (r + 1) * coarse_cols]
        query = jnp.where(own_head, jnp.concatenate([query] * HEADS, axis=0), 0).astype(BF16)
        scores = nt(coarse_keys[r], query)
        coarse_scores[r] = scores
        coarse_top[r] = column_top(scores)

    def coarse_finish(r):
        weights = shifted_weights(coarse_scores[r], coarse_top[r])
        ones = jnp.ones((EDGE, many), BF16)
        mixed = nn(jnp.concatenate([coarse_values[r], ones], axis=0), weights)
        mixed = mixed[:feat] * (1.0 / mixed[feat : feat + 1])
        mixed = jnp.where(diagonal, mixed, 0.0).astype(BF16)
        folded = nt(fold_ref[...], mixed).astype(BF16)
        out = left_coarse_ref[r].astype(F32) + nn(folded, wo_ref[...])
        out = layer_norm(out, gain_ref[...]).astype(BF16)
        ext_ref[r + 1, EDGE : EDGE + coarse_cols] = out
        prior_ref[r] = out

    for r in range(coarse_rows + 2):
        if r == coarse_rows // 2:
            relay(0)
        if r < coarse_rows:
            coarse_project(r)
        if 1 <= r <= coarse_rows:
            coarse_score(r - 1)
        if r >= 2:
            coarse_finish(r - 2)

    def part(d, size, away):
        span = coarse_rows if size is None else coarse_cols
        base = 1 if size is None else EDGE
        pad = 1 if size is None else EDGE
        if d == 0:
            return pl.ds(base, span)
        if away:
            return pl.ds(base if d < 0 else base + span - pad, pad)
        return pl.ds(base + span if d < 0 else base - pad, pad)

    def edge_copy(i):
        dy, dx = sides[i]
        return pltpu.make_async_remote_copy(
            src_ref=ext_ref.at[part(dy, None, True), part(dx, EDGE, True)],
            dst_ref=ext_ref.at[part(dy, None, False), part(dx, EDGE, False)],
            send_sem=edge_send.at[i],
            recv_sem=edge_recv.at[i],
            device_id={"rows": row + dy, "cols": me + dx},
            device_id_type=MESH,
        )

    for i, (dy, dx) in enumerate(sides):

        @pl.when(reach(dy, dx))
        def _(i=i):
            edge_copy(i).start()

    relay(1)

    for i, (dy, dx) in enumerate(sides):

        @pl.when(reach(dy, dx))
        def _(i=i):
            edge_copy(i).wait_send()

        @pl.when(reach(-dy, -dx))
        def _(i=i):
            edge_copy(i).wait_recv()

    last = EDGE + coarse_cols

    @pl.when(me == 0)
    def _():
        ext_ref[:, :EDGE] = jnp.broadcast_to(
            ext_ref[:, EDGE : EDGE + 1], (coarse_rows + 2, EDGE, feat)
        )

    @pl.when(me == n - 1)
    def _():
        ext_ref[:, last:] = jnp.broadcast_to(
            ext_ref[:, last - 1 : last], (coarse_rows + 2, EDGE, feat)
        )

    @pl.when(row == 0)
    def _():
        ext_ref[0] = ext_ref[1]

    @pl.when(row == row_devices - 1)
    def _():
        ext_ref[coarse_rows + 1] = ext_ref[coarse_rows]

    left_copy().wait()

    def query_stage(g):
        coarse = jnp.concatenate([ext_ref[g + i] for i in range(3)], axis=0)
        up = nn(up_ref[...], coarse)
        left = left_ref[pl.ds(g * BAND, BAND)].reshape(up.shape)
        query_in = (left.astype(F32) + up).astype(BF16)
        query_in_ref[g % 2] = query_in
        query_ref[g % 2] = nt(wqt_ref[...], query_in).astype(BF16)

    def out_stage(g):
        product = tn(mix_ref[g % 2], wo_ref[...])
        total = query_in_ref[g % 2].astype(F32) + product
        out = layer_norm(total, gain_ref[...]).astype(BF16)
        fine_ref[pl.ds(g * BAND, BAND)] = out.reshape(BAND, BLOCK, feat)

    def out_copy(g):
        here = pl.ds(g * BAND, BAND)
        return pltpu.make_async_copy(fine_ref.at[here], fine_hbm.at[here], out_sem.at[g])

    query_stage(0)
    query_in_ref[1] = jnp.zeros_like(query_in_ref[1])
    for g in range(2, LEAD):
        relay(g)
    forward(0)

    def branches(g, action):
        for fixed in range(bands):
            pl.when(g == fixed)(functools.partial(action, fixed))

    def enter(g):
        own_copy(g).wait()
        for hop in final_hops(fine_hops):
            fine_copy(g, hop).wait_recv()
        used = count_ref[me, g]
        first = list_ref[me, 0, g]
        for k in range(length):
            pick = first if k == 0 else jnp.where(k < used, list_ref[me, k, g], first)
            picked_ref[:, k * BLOCK : (k + 1) * BLOCK] = bands_ref[g][pick]

    def band_step(g, carry):
        branches(g, enter)
        used = count_ref[me, g]
        lanes = lax.broadcasted_iota(jnp.int32, (1, length * BLOCK), 1)
        live = jnp.where(lanes < used * BLOCK, 1.0, 0.0).astype(BF16)
        ones = jnp.broadcast_to(live, (HEAD_DIM, length * BLOCK))
        now = g % 2

        def prepare(r):
            right = picked_ref[r]
            keys_ref[r] = (nn(right, wk_ref[...]) * KEY_SCALE).astype(BF16)
            values_ref[r] = nt(wvt_ref[...], right).astype(BF16) * live
            for h in range(HEADS):
                rows = slice(h * HEAD_DIM, (h + 1) * HEAD_DIM)
                spread_ref[r, rows, h * BLOCK : (h + 1) * BLOCK] = query_ref[
                    now, rows, r * BLOCK : (r + 1) * BLOCK
                ]

        def score(i):
            r, pair = divmod(i, PAIRS)
            top = None
            for k in range(length):
                keys = keys_ref[r, k * BLOCK : (k + 1) * BLOCK]
                part = nn(keys, spread_ref[r, :, pair * 2 * BLOCK : (pair + 1) * 2 * BLOCK])
                scores_ref[i % SLOTS, k * BLOCK : (k + 1) * BLOCK] = part
                tile = jnp.max(part.reshape(BLOCK // 8, 8, 2 * BLOCK), axis=0)
                top = tile if top is None else jnp.maximum(top, tile)
            top_ref[i % SLOTS] = jnp.broadcast_to(
                jnp.max(top, axis=0, keepdims=True), (8, 2 * BLOCK)
            )

        def process(i):
            r, pair = divmod(i, PAIRS)
            weights = shifted_weights(scores_ref[i % SLOTS], top_ref[i % SLOTS])
            rows = slice(pair * 2 * HEAD_DIM, (pair + 1) * 2 * HEAD_DIM)
            mixed = nn(jnp.concatenate([values_ref[r, rows], ones], axis=0), weights)
            inverse = 1.0 / mixed[2 * HEAD_DIM : 2 * HEAD_DIM + 1]
            here = slice(r * BLOCK, (r + 1) * BLOCK)
            start = pair * 2 * HEAD_DIM
            mix_ref[now, start : start + HEAD_DIM, here] = (
                mixed[:HEAD_DIM, :BLOCK] * inverse[:, :BLOCK]
            ).astype(BF16)
            mix_ref[now, start + HEAD_DIM : start + 2 * HEAD_DIM, here] = (
                mixed[HEAD_DIM : 2 * HEAD_DIM, BLOCK:] * inverse[:, BLOCK:]
            ).astype(BF16)

        prepare(0)
        for i in range(AHEAD):
            score(i)
        out_stage(jnp.maximum(g - 1, 0))
        for i in range(STEPS):
            if i % PAIRS == 0 and i // PAIRS + 1 < BAND:
                prepare(i // PAIRS + 1)
            if i + AHEAD < STEPS:
                score(i + AHEAD)
            process(i)
            if i == RELAY_STEP:
                pl.when(g > 0)(lambda: out_copy(g - 1).start())
                branches(g, lambda fixed: relay(fixed + LEAD))
            if i == FORWARD_STEP:
                branches(g, lambda fixed: forward(fixed + 1))
        query_stage(jnp.minimum(g + 1, bands - 1))
        return carry

    lax.fori_loop(0, bands, band_step, 0)
    out_stage(bands - 1)
    out_copy(bands - 1).start()

    for hop in range(len(start_hops)):
        coarse_copy(hop).wait_send()
    for g in range(bands):
        for hop in range(len(fine_hops)):
            fine_copy(g, hop).wait_send()
        out_copy(g).wait()


def body(
    left_fine,
    right_fine,
    left_coarse,
    right_coarse,
    candidates,
    counts,
    query_weight,
    key_weight,
    value_weight,
    out_weight,
    norm_gain,
):
    n = lax.axis_size("cols")
    rows, cols, feat = left_fine.shape
    bands = rows // BAND
    coarse_rows, coarse_cols, _ = left_coarse.shape
    length = candidates.shape[2]
    up = upsample_matrix(coarse_cols)
    fold = np.tile(np.eye(coarse_cols, dtype=np.float32), (1, HEADS))
    hop_count = len(gather_hops(n, 0))
    many = n * coarse_cols
    wide = HEADS * coarse_cols
    vmem = pl.BlockSpec(memory_space=pltpu.VMEM)
    smem = pl.BlockSpec(memory_space=pltpu.SMEM)
    hbm = pl.BlockSpec(memory_space=pl.ANY)
    return pl.pallas_call(
        functools.partial(kernel, n=n, row_devices=lax.axis_size("rows"), bands=bands),
        out_shape=(
            jax.ShapeDtypeStruct(left_fine.shape, BF16),
            jax.ShapeDtypeStruct(left_coarse.shape, BF16),
        ),
        in_specs=[smem, smem, hbm, hbm] + [vmem] * 9,
        out_specs=(hbm, vmem),
        scratch_shapes=[pltpu.VMEM((n, BAND, cols, feat), BF16) for _ in range(bands)]
        + [
            pltpu.VMEM(left_fine.shape, BF16),
            pltpu.VMEM(left_fine.shape, BF16),
            pltpu.VMEM((n,) + right_coarse.shape, BF16),
            pltpu.VMEM((coarse_rows + 2, coarse_cols + 2 * EDGE, feat), BF16),
            pltpu.VMEM((feat, feat), BF16),
            pltpu.VMEM((feat, feat), BF16),
            pltpu.VMEM((coarse_rows, many, feat), BF16),
            pltpu.VMEM((coarse_rows, feat, many), BF16),
            pltpu.VMEM((coarse_rows * coarse_cols, feat), BF16),
            pltpu.VMEM((coarse_rows, many, wide), F32),
            pltpu.VMEM((coarse_rows, 8, wide), F32),
            pltpu.VMEM((BAND, length * BLOCK, feat), BF16),
            pltpu.VMEM((2, BAND * BLOCK, feat), BF16),
            pltpu.VMEM((2, feat, BAND * BLOCK), BF16),
            pltpu.VMEM((BAND, length * BLOCK, feat), BF16),
            pltpu.VMEM((BAND, feat, length * BLOCK), BF16),
            pltpu.VMEM((BAND, feat, HEADS * BLOCK), BF16),
            pltpu.VMEM((SLOTS, length * BLOCK, 2 * BLOCK), F32),
            pltpu.VMEM((SLOTS, 8, 2 * BLOCK), F32),
            pltpu.VMEM((2, feat, BAND * BLOCK), BF16),
            pltpu.SemaphoreType.DMA((hop_count,)),
            pltpu.SemaphoreType.DMA((hop_count,)),
            pltpu.SemaphoreType.DMA((8,)),
            pltpu.SemaphoreType.DMA((8,)),
            pltpu.SemaphoreType.DMA((bands, hop_count)),
            pltpu.SemaphoreType.DMA((bands, hop_count)),
            pltpu.SemaphoreType.DMA((bands,)),
            pltpu.SemaphoreType.DMA((1,)),
            pltpu.SemaphoreType.DMA((bands,)),
        ],
        compiler_params=pltpu.CompilerParams(
            collective_id=0, has_side_effects=True, vmem_limit_bytes=60 * 1024 * 1024
        ),
        name="stereo",
    )(
        jnp.transpose(candidates, (0, 2, 1)),
        counts,
        left_fine,
        right_fine,
        left_coarse,
        right_coarse,
        jnp.asarray(up, BF16),
        query_weight,
        key_weight,
        value_weight,
        out_weight,
        norm_gain.reshape(1, -1),
        jnp.asarray(fold, BF16),
    )


def solution(mesh):
    return jax.shard_map(
        body,
        mesh=mesh,
        in_specs=(
            P("rows", "cols", None),
            P("rows", "cols", None),
            P("rows", "cols", None),
            P("rows", "cols", None),
            P(None, "rows", None),
            P(None, "rows"),
            P(),
            P(),
            P(),
            P(),
            P(),
        ),
        out_specs=(P("rows", "cols", None), P("rows", "cols", None)),
        check_vma=False,
    )
```

```python
import functools
import math

import jax
import jax.numpy as jnp
import numpy as np
from jax import lax
from jax.experimental import pallas as pl
from jax.experimental.pallas import tpu as pltpu
from jax.sharding import PartitionSpec as P

HEADS = 8
HEAD_DIM = 16
BLOCK = 128
BAND = 4
EPSILON = 1e-05
PAIRS = HEADS // 2
EDGE = 16
LEAD = 3
EARLY = 2
AHEAD = 3
SLOTS = AHEAD + 1
STEPS = BAND * PAIRS
RELAY_STEP = 3
FORWARD_STEP = 9
PARTS = 4
MESH = pl.DeviceIdType.MESH
KEY_SCALE = math.log2(math.e) / math.sqrt(HEAD_DIM)
BF16 = jnp.bfloat16
F32 = jnp.float32


def nt(a, b):
    return lax.dot_general(a, b, (((1,), (1,)), ((), ())), preferred_element_type=F32)


def tn(a, b):
    return lax.dot_general(a, b, (((0,), (0,)), ((), ())), preferred_element_type=F32)


def nn(a, b):
    return jnp.dot(a, b, preferred_element_type=F32)


def layer_norm(values, norm_gain):
    average = jnp.mean(values, axis=-1, keepdims=True)
    centred = values - average
    spread = jnp.mean(centred * centred, axis=-1, keepdims=True)
    return centred * lax.rsqrt(spread + EPSILON) * norm_gain


def upsample_matrix(cols):
    taps = np.array(
        [[0.375, 0.625, 0.0], [0.125, 0.875, 0.0], [0.0, 0.875, 0.125], [0.0, 0.625, 0.375]]
    )
    pitch = cols + 2 * EDGE
    out = np.zeros((BAND, cols, 4, 3, pitch), np.float32)
    for c in range(cols):
        for t in range(4):
            for d in range(3):
                out[:, c, t, :, c + d + EDGE - 1] = taps[:, :] * taps[t, d]
    return out.reshape(BAND * cols * 4, 3 * pitch)


def flipped(index, bit):
    return index + bit - 2 * bit * ((index // bit) % 2)


def gather_hops(n, me):
    if n != 8:
        return [(me, (me + j) % n, None) for j in range(1, n)]
    a, b, c = flipped(me, 1), flipped(me, 2), flipped(me, 4)
    d = flipped(b, 4)
    odd = me % 2
    relay_block = b + odd * (c - b)
    relay_target = c + odd * (b - c)
    return [
        (me, b, None),
        (me, c, None),
        (me, a, None),
        (relay_block, relay_target, (0, 1)),
        (b, a, (0,)),
        (c, a, (1,)),
        (d, a, (3,)),
    ]


def coarse_hops(n, me):
    if n != 8:
        return [(me, (me + j) % n, None) for j in range(1, n)]
    a, b, c = flipped(me, 1), flipped(me, 2), flipped(me, 4)
    d = flipped(b, 4)
    return [
        (me, b, None),
        (me, c, None),
        (me, d, None),
        (me, a, None),
        (b, a, (0,)),
        (c, a, (1,)),
        (d, a, (2,)),
    ]


def hop_levels(hops):
    levels = []
    for hop in hops:
        levels.append(0 if hop[2] is None else 1 + max(levels[i] for i in hop[2]))
    return levels


def final_hops(hops):
    used = {i for hop in hops for i in hop[2] or ()}
    return [i for i in range(len(hops)) if i not in used]


def column_top(scores):
    rows, cols = scores.shape
    tile = jnp.max(scores.reshape(rows // 8, 8, cols), axis=0)
    return jnp.broadcast_to(jnp.max(tile, axis=0, keepdims=True), (8, cols))


def shifted_weights(scores, top):
    rows, cols = scores.shape
    shifted = scores.reshape(rows // 8, 8, cols) - top[None]
    return jnp.exp2(shifted.reshape(rows, cols).astype(BF16))


def kernel(
    list_ref,
    count_ref,
    left_hbm,
    right_ref,
    left_coarse_ref,
    right_coarse_ref,
    up_ref,
    wq_ref,
    wk_ref,
    wv_ref,
    wo_ref,
    gain_ref,
    fold_ref,
    fine_hbm,
    prior_ref,
    *scratch,
    n,
    row_devices,
    bands,
):
    bands_ref = scratch[:bands]
    (
        left_ref,
        fine_ref,
        coarse_ref,
        ext_ref,
        wqt_ref,
        wvt_ref,
        coarse_keys,
        coarse_values,
        coarse_query,
        coarse_scores,
        coarse_top,
        picked_ref,
        query_in_ref,
        query_ref,
        keys_ref,
        values_ref,
        spread_ref,
        scores_ref,
        top_ref,
        mix_ref,
        coarse_send,
        coarse_recv,
        edge_send,
        edge_recv,
        fine_send,
        fine_recv,
        own_sem,
        left_sem,
        out_sem,
    ) = scratch[bands:]
    me = lax.axis_index("cols")
    row = lax.axis_index("rows")
    coarse_rows, coarse_cols, feat = left_coarse_ref.shape
    length = list_ref.shape[1]
    fine_hops = gather_hops(n, me)
    start_hops = coarse_hops(n, me)

    inside = {
        -1: (row > 0, me > 0),
        0: (True, True),
        1: (row < row_devices - 1, me < n - 1),
    }
    sides = [(dy, dx) for dy in (-1, 0, 1) for dx in (-1, 0, 1) if dy or dx]

    def reach(dy, dx):
        return jnp.logical_and(inside[dy][0], inside[dx][1])

    barrier = pltpu.get_barrier_semaphore()
    for j in range(1, n):
        pl.semaphore_signal(
            barrier, inc=1, device_id={"cols": (me + j) % n}, device_id_type=MESH
        )
    expected = n - 1
    for dy, dx in sides:
        if dy:
            there = reach(dy, dx)

            @pl.when(there)
            def _(dy=dy, dx=dx):
                pl.semaphore_signal(
                    barrier,
                    inc=1,
                    device_id={"rows": row + dy, "cols": me + dx},
                    device_id_type=MESH,
                )

            expected = expected + there.astype(jnp.int32)

    def left_copy():
        return pltpu.make_async_copy(left_hbm, left_ref, left_sem.at[0])

    def own_copy(g):
        return pltpu.make_async_copy(
            right_ref.at[pl.ds(g * BAND, BAND)], bands_ref[g].at[me], own_sem.at[g]
        )

    left_copy().start()
    for g in range(bands):
        own_copy(g).start()
    pl.semaphore_wait(barrier, expected)

    def coarse_copy(hop):
        block, target, after = start_hops[hop]
        return pltpu.make_async_remote_copy(
            src_ref=right_coarse_ref if after is None else coarse_ref.at[block],
            dst_ref=coarse_ref.at[block],
            send_sem=coarse_send.at[hop],
            recv_sem=coarse_recv.at[hop],
            device_id={"cols": target},
            device_id_type=MESH,
        )

    def fine_copy(g, hop):
        block, target, after = fine_hops[hop]
        if after is None:
            source = right_ref.at[pl.ds(g * BAND, BAND)]
        else:
            source = bands_ref[g].at[block]
        return pltpu.make_async_remote_copy(
            src_ref=source,
            dst_ref=bands_ref[g].at[block],
            send_sem=fine_send.at[g, hop],
            recv_sem=fine_recv.at[g, hop],
            device_id={"cols": target},
            device_id_type=MESH,
        )

    def send(copy, hops, level):
        levels = hop_levels(hops)
        ready = set()
        for hop in range(len(hops)):
            if levels[hop] == level:
                for needed in hops[hop][2] or ():
                    if needed not in ready and levels[needed] == level - 1:
                        ready.add(needed)
                        copy(needed).wait_recv()
                copy(hop).start()

    def send_fine(g, level):
        if 0 <= g < bands:
            send(functools.partial(fine_copy, g), fine_hops, level)

    fine_depth = max(hop_levels(fine_hops))
    coarse_depth = max(hop_levels(start_hops))

    send(coarse_copy, start_hops, 0)
    for g in range(EARLY):
        send_fine(g, 0)
    coarse_ref[me] = right_coarse_ref[...]
    wqt_ref[...] = wq_ref[...].T
    wvt_ref[...] = wv_ref[...].T
    spread_ref[...] = jnp.zeros_like(spread_ref)
    mix_ref[...] = jnp.zeros_like(mix_ref)
    left_all = left_coarse_ref[...].reshape(coarse_rows * coarse_cols, feat)
    coarse_query[...] = nn(left_all, wq_ref[...]).astype(BF16)
    for level in range(1, coarse_depth + 1):
        send(coarse_copy, start_hops, level)
    for g in range(EARLY, LEAD):
        send_fine(g, 0)
    for hop in final_hops(start_hops):
        coarse_copy(hop).wait_recv()

    def relay(g):
        send_fine(g, 1)
        send_fine(g + LEAD, 0)

    def forward(g):
        for level in range(2, fine_depth + 1):
            send_fine(g, level)

    wide = HEADS * coarse_cols
    many = n * coarse_cols
    own_head = (
        lax.broadcasted_iota(jnp.int32, (wide, feat), 0) // coarse_cols
        == lax.broadcasted_iota(jnp.int32, (wide, feat), 1) // HEAD_DIM
    )
    diagonal = (
        lax.broadcasted_iota(jnp.int32, (feat, wide), 0) // HEAD_DIM
        == lax.broadcasted_iota(jnp.int32, (feat, wide), 1) // coarse_cols
    )

    def coarse_project(r):
        right = coarse_ref[:, r].reshape(many, feat)
        coarse_keys[r] = (nn(right, wk_ref[...]) * KEY_SCALE).astype(BF16)
        coarse_values[r] = nt(wvt_ref[...], right).astype(BF16)

    def coarse_score(r):
        query = coarse_query[r * coarse_cols : (r + 1) * coarse_cols]
        query = jnp.where(own_head, jnp.concatenate([query] * HEADS, axis=0), 0).astype(BF16)
        scores = nt(coarse_keys[r], query)
        coarse_scores[r] = scores
        coarse_top[r] = column_top(scores)

    def coarse_finish(r):
        weights = shifted_weights(coarse_scores[r], coarse_top[r])
        ones = jnp.ones((EDGE, many), BF16)
        mixed = nn(jnp.concatenate([coarse_values[r], ones], axis=0), weights)
        mixed = mixed[:feat] * (1.0 / mixed[feat : feat + 1])
        mixed = jnp.where(diagonal, mixed, 0.0).astype(BF16)
        folded = nt(fold_ref[...], mixed).astype(BF16)
        out = left_coarse_ref[r].astype(F32) + nn(folded, wo_ref[...])
        out = layer_norm(out, gain_ref[...]).astype(BF16)
        ext_ref[r + 1, EDGE : EDGE + coarse_cols] = out
        prior_ref[r] = out

    for r in range(coarse_rows + 2):
        if r == coarse_rows // 2:
            relay(0)
        if r < coarse_rows:
            coarse_project(r)
        if 1 <= r <= coarse_rows:
            coarse_score(r - 1)
        if r >= 2:
            coarse_finish(r - 2)

    def part(d, size, away):
        span = coarse_rows if size is None else coarse_cols
        base = 1 if size is None else EDGE
        pad = 1 if size is None else EDGE
        if d == 0:
            return pl.ds(base, span)
        if away:
            return pl.ds(base if d < 0 else base + span - pad, pad)
        return pl.ds(base + span if d < 0 else base - pad, pad)

    def edge_copy(i):
        dy, dx = sides[i]
        return pltpu.make_async_remote_copy(
            src_ref=ext_ref.at[part(dy, None, True), part(dx, EDGE, True)],
            dst_ref=ext_ref.at[part(dy, None, False), part(dx, EDGE, False)],
            send_sem=edge_send.at[i],
            recv_sem=edge_recv.at[i],
            device_id={"rows": row + dy, "cols": me + dx},
            device_id_type=MESH,
        )

    for i, (dy, dx) in enumerate(sides):

        @pl.when(reach(dy, dx))
        def _(i=i):
            edge_copy(i).start()

    relay(1)

    for i, (dy, dx) in enumerate(sides):

        @pl.when(reach(dy, dx))
        def _(i=i):
            edge_copy(i).wait_send()

        @pl.when(reach(-dy, -dx))
        def _(i=i):
            edge_copy(i).wait_recv()

    last = EDGE + coarse_cols

    @pl.when(me == 0)
    def _():
        ext_ref[:, :EDGE] = jnp.broadcast_to(
            ext_ref[:, EDGE : EDGE + 1], (coarse_rows + 2, EDGE, feat)
        )

    @pl.when(me == n - 1)
    def _():
        ext_ref[:, last:] = jnp.broadcast_to(
            ext_ref[:, last - 1 : last], (coarse_rows + 2, EDGE, feat)
        )

    @pl.when(row == 0)
    def _():
        ext_ref[0] = ext_ref[1]

    @pl.when(row == row_devices - 1)
    def _():
        ext_ref[coarse_rows + 1] = ext_ref[coarse_rows]

    left_copy().wait()

    def query_stage(g):
        coarse = jnp.concatenate([ext_ref[g + i] for i in range(3)], axis=0)
        up = nn(up_ref[...], coarse)
        left = left_ref[pl.ds(g * BAND, BAND)].reshape(up.shape)
        query_in = (left.astype(F32) + up).astype(BF16)
        query_in_ref[g % 2] = query_in
        query_ref[g % 2] = nt(wqt_ref[...], query_in).astype(BF16)

    def out_stage(g):
        product = tn(mix_ref[g % 2], wo_ref[...])
        total = query_in_ref[g % 2].astype(F32) + product
        out = layer_norm(total, gain_ref[...]).astype(BF16)
        fine_ref[pl.ds(g * BAND, BAND)] = out.reshape(BAND, BLOCK, feat)

    def out_copy(g):
        here = pl.ds(g * BAND, BAND)
        return pltpu.make_async_copy(fine_ref.at[here], fine_hbm.at[here], out_sem.at[g])

    query_stage(0)
    query_in_ref[1] = jnp.zeros_like(query_in_ref[1])
    for g in range(2, LEAD):
        relay(g)
    forward(0)

    def branches(g, action):
        for fixed in range(bands):
            pl.when(g == fixed)(functools.partial(action, fixed))

    def enter(g):
        own_copy(g).wait()
        for hop in final_hops(fine_hops):
            fine_copy(g, hop).wait_recv()
        used = count_ref[me, g]
        first = list_ref[me, 0, g]
        for k in range(length):
            pick = first if k == 0 else jnp.where(k < used, list_ref[me, k, g], first)
            picked_ref[:, k * BLOCK : (k + 1) * BLOCK] = bands_ref[g][pick]

    def band_step(g, carry):
        branches(g, enter)
        used = count_ref[me, g]
        lanes = lax.broadcasted_iota(jnp.int32, (1, length * BLOCK), 1)
        live = jnp.where(lanes < used * BLOCK, 1.0, 0.0).astype(BF16)
        ones = jnp.broadcast_to(live, (HEAD_DIM, length * BLOCK))
        now = g % 2

        def prepare(r):
            right = picked_ref[r]
            keys_ref[r] = (nn(right, wk_ref[...]) * KEY_SCALE).astype(BF16)
            values_ref[r] = nt(wvt_ref[...], right).astype(BF16) * live
            for h in range(HEADS):
                rows = slice(h * HEAD_DIM, (h + 1) * HEAD_DIM)
                spread_ref[r, rows, h * BLOCK : (h + 1) * BLOCK] = query_ref[
                    now, rows, r * BLOCK : (r + 1) * BLOCK
                ]

        def score(i):
            r, pair = divmod(i, PAIRS)
            top = None
            for k in range(length):
                keys = keys_ref[r, k * BLOCK : (k + 1) * BLOCK]
                part = nn(keys, spread_ref[r, :, pair * 2 * BLOCK : (pair + 1) * 2 * BLOCK])
                scores_ref[i % SLOTS, k * BLOCK : (k + 1) * BLOCK] = part
                tile = jnp.max(part.reshape(BLOCK // 8, 8, 2 * BLOCK), axis=0)
                top = tile if top is None else jnp.maximum(top, tile)
            top_ref[i % SLOTS] = jnp.broadcast_to(
                jnp.max(top, axis=0, keepdims=True), (8, 2 * BLOCK)
            )

        def process(i):
            r, pair = divmod(i, PAIRS)
            weights = shifted_weights(scores_ref[i % SLOTS], top_ref[i % SLOTS])
            rows = slice(pair * 2 * HEAD_DIM, (pair + 1) * 2 * HEAD_DIM)
            mixed = nn(jnp.concatenate([values_ref[r, rows], ones], axis=0), weights)
            inverse = 1.0 / mixed[2 * HEAD_DIM : 2 * HEAD_DIM + 1]
            here = slice(r * BLOCK, (r + 1) * BLOCK)
            start = pair * 2 * HEAD_DIM
            mix_ref[now, start : start + HEAD_DIM, here] = (
                mixed[:HEAD_DIM, :BLOCK] * inverse[:, :BLOCK]
            ).astype(BF16)
            mix_ref[now, start + HEAD_DIM : start + 2 * HEAD_DIM, here] = (
                mixed[HEAD_DIM : 2 * HEAD_DIM, BLOCK:] * inverse[:, BLOCK:]
            ).astype(BF16)

        prepare(0)
        for i in range(AHEAD):
            score(i)
        out_stage(jnp.maximum(g - 1, 0))
        for i in range(STEPS):
            if i % PAIRS == 0 and i // PAIRS + 1 < BAND:
                prepare(i // PAIRS + 1)
            if i + AHEAD < STEPS:
                score(i + AHEAD)
            process(i)
            if i == RELAY_STEP:
                pl.when(g > 0)(lambda: out_copy(g - 1).start())
                branches(g, lambda fixed: relay(fixed + LEAD))
            if i == FORWARD_STEP:
                branches(g, lambda fixed: forward(fixed + 1))
        query_stage(jnp.minimum(g + 1, bands - 1))
        return carry

    lax.fori_loop(0, bands, band_step, 0)
    out_stage(bands - 1)
    out_copy(bands - 1).start()

    for hop in range(len(start_hops)):
        coarse_copy(hop).wait_send()
    for g in range(bands):
        for hop in range(len(fine_hops)):
            fine_copy(g, hop).wait_send()
        out_copy(g).wait()


def finish_kernel(fine_ref, prior_ref, fine_out, prior_out, fine_buf, prior_buf, into, out_of):
    parts = into.shape[0] - 1
    size = fine_ref.shape[0] // parts
    steps = [
        (fine_ref.at[here], fine_buf.at[here], fine_out.at[here])
        for here in (pl.ds(i * size, size) for i in range(parts))
    ]
    steps.append((prior_ref, prior_buf, prior_out))
    loads = [
        pltpu.make_async_copy(source, held, into.at[i]) for i, (source, held, _) in enumerate(steps)
    ]
    stores = [
        pltpu.make_async_copy(held, target, out_of.at[i])
        for i, (_, held, target) in enumerate(steps)
    ]
    for load in loads:
        load.start()
    for load, store in zip(loads, stores):
        load.wait()
        store.start()
    for store in stores:
        store.wait()


def finish(fine, prior):
    hbm = pl.BlockSpec(memory_space=pl.ANY)
    parts = min(PARTS, fine.shape[0])
    return pl.pallas_call(
        finish_kernel,
        out_shape=(
            jax.ShapeDtypeStruct(fine.shape, BF16),
            jax.ShapeDtypeStruct(prior.shape, BF16),
        ),
        in_specs=[hbm, hbm],
        out_specs=(hbm, hbm),
        scratch_shapes=[
            pltpu.VMEM(fine.shape, BF16),
            pltpu.VMEM(prior.shape, BF16),
            pltpu.SemaphoreType.DMA((parts + 1,)),
            pltpu.SemaphoreType.DMA((parts + 1,)),
        ],
        compiler_params=pltpu.CompilerParams(vmem_limit_bytes=60 * 1024 * 1024),
        name="finish",
    )(fine, prior)


def body(
    left_fine,
    right_fine,
    left_coarse,
    right_coarse,
    candidates,
    counts,
    query_weight,
    key_weight,
    value_weight,
    out_weight,
    norm_gain,
):
    n = lax.axis_size("cols")
    rows, cols, feat = left_fine.shape
    bands = rows // BAND
    coarse_rows, coarse_cols, _ = left_coarse.shape
    length = candidates.shape[2]
    up = upsample_matrix(coarse_cols)
    fold = np.tile(np.eye(coarse_cols, dtype=np.float32), (1, HEADS))
    hop_count = len(gather_hops(n, 0))
    many = n * coarse_cols
    wide = HEADS * coarse_cols
    vmem = pl.BlockSpec(memory_space=pltpu.VMEM)
    smem = pl.BlockSpec(memory_space=pltpu.SMEM)
    hbm = pl.BlockSpec(memory_space=pl.ANY)
    out = pl.pallas_call(
        functools.partial(kernel, n=n, row_devices=lax.axis_size("rows"), bands=bands),
        out_shape=(
            jax.ShapeDtypeStruct(left_fine.shape, BF16),
            jax.ShapeDtypeStruct(left_coarse.shape, BF16),
        ),
        in_specs=[smem, smem, hbm, hbm] + [vmem] * 9,
        out_specs=(hbm, vmem),
        scratch_shapes=[pltpu.VMEM((n, BAND, cols, feat), BF16) for _ in range(bands)]
        + [
            pltpu.VMEM(left_fine.shape, BF16),
            pltpu.VMEM(left_fine.shape, BF16),
            pltpu.VMEM((n,) + right_coarse.shape, BF16),
            pltpu.VMEM((coarse_rows + 2, coarse_cols + 2 * EDGE, feat), BF16),
            pltpu.VMEM((feat, feat), BF16),
            pltpu.VMEM((feat, feat), BF16),
            pltpu.VMEM((coarse_rows, many, feat), BF16),
            pltpu.VMEM((coarse_rows, feat, many), BF16),
            pltpu.VMEM((coarse_rows * coarse_cols, feat), BF16),
            pltpu.VMEM((coarse_rows, many, wide), F32),
            pltpu.VMEM((coarse_rows, 8, wide), F32),
            pltpu.VMEM((BAND, length * BLOCK, feat), BF16),
            pltpu.VMEM((2, BAND * BLOCK, feat), BF16),
            pltpu.VMEM((2, feat, BAND * BLOCK), BF16),
            pltpu.VMEM((BAND, length * BLOCK, feat), BF16),
            pltpu.VMEM((BAND, feat, length * BLOCK), BF16),
            pltpu.VMEM((BAND, feat, HEADS * BLOCK), BF16),
            pltpu.VMEM((SLOTS, length * BLOCK, 2 * BLOCK), F32),
            pltpu.VMEM((SLOTS, 8, 2 * BLOCK), F32),
            pltpu.VMEM((2, feat, BAND * BLOCK), BF16),
            pltpu.SemaphoreType.DMA((hop_count,)),
            pltpu.SemaphoreType.DMA((hop_count,)),
            pltpu.SemaphoreType.DMA((8,)),
            pltpu.SemaphoreType.DMA((8,)),
            pltpu.SemaphoreType.DMA((bands, hop_count)),
            pltpu.SemaphoreType.DMA((bands, hop_count)),
            pltpu.SemaphoreType.DMA((bands,)),
            pltpu.SemaphoreType.DMA((1,)),
            pltpu.SemaphoreType.DMA((bands,)),
        ],
        compiler_params=pltpu.CompilerParams(
            collective_id=0, has_side_effects=True, vmem_limit_bytes=60 * 1024 * 1024
        ),
        name="stereo",
    )(
        jnp.transpose(candidates, (0, 2, 1)),
        counts,
        left_fine,
        right_fine,
        left_coarse,
        right_coarse,
        jnp.asarray(up, BF16),
        query_weight,
        key_weight,
        value_weight,
        out_weight,
        norm_gain.reshape(1, -1),
        jnp.asarray(fold, BF16),
    )
    return finish(*out)


def solution(mesh):
    return jax.shard_map(
        body,
        mesh=mesh,
        in_specs=(
            P("rows", "cols", None),
            P("rows", "cols", None),
            P("rows", "cols", None),
            P("rows", "cols", None),
            P(None, "rows", None),
            P(None, "rows"),
            P(),
            P(),
            P(),
            P(),
            P(),
        ),
        out_specs=(P("rows", "cols", None), P("rows", "cols", None)),
        check_vma=False,
    )
```

```python
import functools
import math

import jax
import jax.numpy as jnp
import numpy as np
from jax import lax
from jax.experimental import pallas as pl
from jax.experimental.pallas import tpu as pltpu
from jax.sharding import PartitionSpec as P

HEADS = 8
HEAD_DIM = 16
BLOCK = 128
BAND = 4
EPSILON = 1e-05
PAIRS = HEADS // 2
EDGE = 16
LEAD = 2
EARLY = 2
AHEAD = 3
SLOTS = AHEAD + 1
STEPS = BAND * PAIRS
RELAY_STEP = 1
FORWARD_STEP = 7
PARTS = 4
MESH = pl.DeviceIdType.MESH
KEY_SCALE = math.log2(math.e) / math.sqrt(HEAD_DIM)
BF16 = jnp.bfloat16
F32 = jnp.float32


def nt(a, b):
    return lax.dot_general(a, b, (((1,), (1,)), ((), ())), preferred_element_type=F32)


def tn(a, b):
    return lax.dot_general(a, b, (((0,), (0,)), ((), ())), preferred_element_type=F32)


def nn(a, b):
    return jnp.dot(a, b, preferred_element_type=F32)


def layer_norm(values, norm_gain):
    average = jnp.mean(values, axis=-1, keepdims=True)
    centred = values - average
    spread = jnp.mean(centred * centred, axis=-1, keepdims=True)
    return centred * lax.rsqrt(spread + EPSILON) * norm_gain


def upsample_matrix(cols):
    taps = np.array(
        [[0.375, 0.625, 0.0], [0.125, 0.875, 0.0], [0.0, 0.875, 0.125], [0.0, 0.625, 0.375]]
    )
    pitch = cols + 2 * EDGE
    out = np.zeros((BAND, cols, 4, 3, pitch), np.float32)
    for c in range(cols):
        for t in range(4):
            for d in range(3):
                out[:, c, t, :, c + d + EDGE - 1] = taps[:, :] * taps[t, d]
    return out.reshape(BAND * cols * 4, 3 * pitch)


def flipped(index, bit):
    return index + bit - 2 * bit * ((index // bit) % 2)


def gather_hops(n, me):
    if n != 8:
        return [(me, (me + j) % n, None) for j in range(1, n)]
    a, b, c = flipped(me, 1), flipped(me, 2), flipped(me, 4)
    d = flipped(b, 4)
    odd = me % 2
    relay_block = b + odd * (c - b)
    relay_target = c + odd * (b - c)
    return [
        (me, b, None),
        (me, c, None),
        (me, a, None),
        (relay_block, relay_target, (0, 1)),
        (b, a, (0,)),
        (c, a, (1,)),
        (d, a, (3,)),
    ]


def coarse_hops(n, me):
    if n != 8:
        return [(me, (me + j) % n, None) for j in range(1, n)]
    a, b, c = flipped(me, 1), flipped(me, 2), flipped(me, 4)
    d = flipped(b, 4)
    return [
        (me, b, None),
        (me, c, None),
        (me, d, None),
        (me, a, None),
        (b, a, (0,)),
        (c, a, (1,)),
        (d, a, (2,)),
    ]


def hop_levels(hops):
    levels = []
    for hop in hops:
        levels.append(0 if hop[2] is None else 1 + max(levels[i] for i in hop[2]))
    return levels


def final_hops(hops):
    used = {i for hop in hops for i in hop[2] or ()}
    return [i for i in range(len(hops)) if i not in used]


def column_top(scores):
    rows, cols = scores.shape
    tile = jnp.max(scores.reshape(rows // 8, 8, cols), axis=0)
    return jnp.broadcast_to(jnp.max(tile, axis=0, keepdims=True), (8, cols))


def shifted_weights(scores, top):
    rows, cols = scores.shape
    shifted = scores.reshape(rows // 8, 8, cols) - top[None]
    return jnp.exp2(shifted.reshape(rows, cols).astype(BF16))


def kernel(
    list_ref,
    count_ref,
    left_hbm,
    right_ref,
    left_coarse_ref,
    right_coarse_ref,
    up_ref,
    wq_ref,
    wk_ref,
    wv_ref,
    wo_ref,
    gain_ref,
    fold_ref,
    fine_hbm,
    prior_ref,
    *scratch,
    n,
    row_devices,
    bands,
):
    bands_ref = scratch[:bands]
    (
        left_ref,
        fine_ref,
        coarse_ref,
        ext_ref,
        wqt_ref,
        wvt_ref,
        coarse_keys,
        coarse_values,
        coarse_query,
        coarse_scores,
        coarse_top,
        picked_ref,
        query_in_ref,
        query_ref,
        keys_ref,
        values_ref,
        spread_ref,
        scores_ref,
        top_ref,
        mix_ref,
        coarse_send,
        coarse_recv,
        edge_send,
        edge_recv,
        fine_send,
        fine_recv,
        own_sem,
        left_sem,
        out_sem,
    ) = scratch[bands:]
    me = lax.axis_index("cols")
    row = lax.axis_index("rows")
    coarse_rows, coarse_cols, feat = left_coarse_ref.shape
    length = list_ref.shape[1]
    fine_hops = gather_hops(n, me)
    start_hops = coarse_hops(n, me)

    inside = {
        -1: (row > 0, me > 0),
        0: (True, True),
        1: (row < row_devices - 1, me < n - 1),
    }
    sides = [(dy, dx) for dy in (-1, 0, 1) for dx in (-1, 0, 1) if dy or dx]

    def reach(dy, dx):
        return jnp.logical_and(inside[dy][0], inside[dx][1])

    barrier = pltpu.get_barrier_semaphore()
    for j in range(1, n):
        pl.semaphore_signal(
            barrier, inc=1, device_id={"cols": (me + j) % n}, device_id_type=MESH
        )
    expected = n - 1
    for dy, dx in sides:
        if dy:
            there = reach(dy, dx)

            @pl.when(there)
            def _(dy=dy, dx=dx):
                pl.semaphore_signal(
                    barrier,
                    inc=1,
                    device_id={"rows": row + dy, "cols": me + dx},
                    device_id_type=MESH,
                )

            expected = expected + there.astype(jnp.int32)

    def left_copy():
        return pltpu.make_async_copy(left_hbm, left_ref, left_sem.at[0])

    def own_copy(g):
        return pltpu.make_async_copy(
            right_ref.at[pl.ds(g * BAND, BAND)], bands_ref[g].at[me], own_sem.at[g]
        )

    left_copy().start()
    for g in range(bands):
        own_copy(g).start()
    pl.semaphore_wait(barrier, expected)

    def coarse_copy(hop):
        block, target, after = start_hops[hop]
        return pltpu.make_async_remote_copy(
            src_ref=right_coarse_ref if after is None else coarse_ref.at[block],
            dst_ref=coarse_ref.at[block],
            send_sem=coarse_send.at[hop],
            recv_sem=coarse_recv.at[hop],
            device_id={"cols": target},
            device_id_type=MESH,
        )

    def fine_copy(g, hop):
        block, target, after = fine_hops[hop]
        if after is None:
            source = right_ref.at[pl.ds(g * BAND, BAND)]
        else:
            source = bands_ref[g].at[block]
        return pltpu.make_async_remote_copy(
            src_ref=source,
            dst_ref=bands_ref[g].at[block],
            send_sem=fine_send.at[g, hop],
            recv_sem=fine_recv.at[g, hop],
            device_id={"cols": target},
            device_id_type=MESH,
        )

    def send(copy, hops, level):
        levels = hop_levels(hops)
        ready = set()
        for hop in range(len(hops)):
            if levels[hop] == level:
                for needed in hops[hop][2] or ():
                    if needed not in ready and levels[needed] == level - 1:
                        ready.add(needed)
                        copy(needed).wait_recv()
                copy(hop).start()

    def send_fine(g, level):
        if 0 <= g < bands:
            send(functools.partial(fine_copy, g), fine_hops, level)

    fine_depth = max(hop_levels(fine_hops))
    coarse_depth = max(hop_levels(start_hops))

    send(coarse_copy, start_hops, 0)
    for g in range(EARLY):
        send_fine(g, 0)
    coarse_ref[me] = right_coarse_ref[...]
    wqt_ref[...] = wq_ref[...].T
    wvt_ref[...] = wv_ref[...].T
    spread_ref[...] = jnp.zeros_like(spread_ref)
    mix_ref[...] = jnp.zeros_like(mix_ref)
    left_all = left_coarse_ref[...].reshape(coarse_rows * coarse_cols, feat)
    coarse_query[...] = nn(left_all, wq_ref[...]).astype(BF16)
    for level in range(1, coarse_depth + 1):
        send(coarse_copy, start_hops, level)
    for g in range(EARLY, LEAD):
        send_fine(g, 0)
    for hop in final_hops(start_hops):
        coarse_copy(hop).wait_recv()

    def relay(g):
        send_fine(g, 1)
        send_fine(g + LEAD, 0)

    def forward(g):
        for level in range(2, fine_depth + 1):
            send_fine(g, level)

    wide = HEADS * coarse_cols
    many = n * coarse_cols
    own_head = (
        lax.broadcasted_iota(jnp.int32, (wide, feat), 0) // coarse_cols
        == lax.broadcasted_iota(jnp.int32, (wide, feat), 1) // HEAD_DIM
    )
    diagonal = (
        lax.broadcasted_iota(jnp.int32, (feat, wide), 0) // HEAD_DIM
        == lax.broadcasted_iota(jnp.int32, (feat, wide), 1) // coarse_cols
    )

    def coarse_project(r):
        right = coarse_ref[:, r].reshape(many, feat)
        coarse_keys[r] = (nn(right, wk_ref[...]) * KEY_SCALE).astype(BF16)
        coarse_values[r] = nt(wvt_ref[...], right).astype(BF16)

    def coarse_score(r):
        query = coarse_query[r * coarse_cols : (r + 1) * coarse_cols]
        query = jnp.where(own_head, jnp.concatenate([query] * HEADS, axis=0), 0).astype(BF16)
        scores = nt(coarse_keys[r], query)
        coarse_scores[r] = scores
        coarse_top[r] = column_top(scores)

    def coarse_finish(r):
        weights = shifted_weights(coarse_scores[r], coarse_top[r])
        ones = jnp.ones((EDGE, many), BF16)
        mixed = nn(jnp.concatenate([coarse_values[r], ones], axis=0), weights)
        mixed = mixed[:feat] * (1.0 / mixed[feat : feat + 1])
        mixed = jnp.where(diagonal, mixed, 0.0).astype(BF16)
        folded = nt(fold_ref[...], mixed).astype(BF16)
        out = left_coarse_ref[r].astype(F32) + nn(folded, wo_ref[...])
        out = layer_norm(out, gain_ref[...]).astype(BF16)
        ext_ref[r + 1, EDGE : EDGE + coarse_cols] = out
        prior_ref[r] = out

    for r in range(coarse_rows + 2):
        if r == coarse_rows // 2:
            relay(0)
        if r < coarse_rows:
            coarse_project(r)
        if 1 <= r <= coarse_rows:
            coarse_score(r - 1)
        if r >= 2:
            coarse_finish(r - 2)

    def part(d, size, away):
        span = coarse_rows if size is None else coarse_cols
        base = 1 if size is None else EDGE
        pad = 1 if size is None else EDGE
        if d == 0:
            return pl.ds(base, span)
        if away:
            return pl.ds(base if d < 0 else base + span - pad, pad)
        return pl.ds(base + span if d < 0 else base - pad, pad)

    def edge_copy(i):
        dy, dx = sides[i]
        return pltpu.make_async_remote_copy(
            src_ref=ext_ref.at[part(dy, None, True), part(dx, EDGE, True)],
            dst_ref=ext_ref.at[part(dy, None, False), part(dx, EDGE, False)],
            send_sem=edge_send.at[i],
            recv_sem=edge_recv.at[i],
            device_id={"rows": row + dy, "cols": me + dx},
            device_id_type=MESH,
        )

    for i, (dy, dx) in enumerate(sides):

        @pl.when(reach(dy, dx))
        def _(i=i):
            edge_copy(i).start()

    relay(1)

    for i, (dy, dx) in enumerate(sides):

        @pl.when(reach(dy, dx))
        def _(i=i):
            edge_copy(i).wait_send()

        @pl.when(reach(-dy, -dx))
        def _(i=i):
            edge_copy(i).wait_recv()

    last = EDGE + coarse_cols

    @pl.when(me == 0)
    def _():
        ext_ref[:, :EDGE] = jnp.broadcast_to(
            ext_ref[:, EDGE : EDGE + 1], (coarse_rows + 2, EDGE, feat)
        )

    @pl.when(me == n - 1)
    def _():
        ext_ref[:, last:] = jnp.broadcast_to(
            ext_ref[:, last - 1 : last], (coarse_rows + 2, EDGE, feat)
        )

    @pl.when(row == 0)
    def _():
        ext_ref[0] = ext_ref[1]

    @pl.when(row == row_devices - 1)
    def _():
        ext_ref[coarse_rows + 1] = ext_ref[coarse_rows]

    left_copy().wait()

    def query_stage(g):
        coarse = jnp.concatenate([ext_ref[g + i] for i in range(3)], axis=0)
        up = nn(up_ref[...], coarse)
        left = left_ref[pl.ds(g * BAND, BAND)].reshape(up.shape)
        query_in = (left.astype(F32) + up).astype(BF16)
        query_in_ref[g % 2] = query_in
        query_ref[g % 2] = nt(wqt_ref[...], query_in).astype(BF16)

    def out_stage(g):
        product = tn(mix_ref[g % 2], wo_ref[...])
        total = query_in_ref[g % 2].astype(F32) + product
        out = layer_norm(total, gain_ref[...]).astype(BF16)
        fine_ref[pl.ds(g * BAND, BAND)] = out.reshape(BAND, BLOCK, feat)

    def out_copy(g):
        here = pl.ds(g * BAND, BAND)
        return pltpu.make_async_copy(fine_ref.at[here], fine_hbm.at[here], out_sem.at[g])

    query_stage(0)
    query_in_ref[1] = jnp.zeros_like(query_in_ref[1])
    for g in range(2, LEAD):
        relay(g)
    forward(0)

    def branches(g, action):
        for fixed in range(bands):
            pl.when(g == fixed)(functools.partial(action, fixed))

    def enter(g):
        own_copy(g).wait()
        for hop in final_hops(fine_hops):
            fine_copy(g, hop).wait_recv()
        used = count_ref[me, g]
        first = list_ref[me, 0, g]
        for k in range(length):
            pick = first if k == 0 else jnp.where(k < used, list_ref[me, k, g], first)
            picked_ref[:, k * BLOCK : (k + 1) * BLOCK] = bands_ref[g][pick]

    def band_step(g, carry):
        branches(g, enter)
        used = count_ref[me, g]
        lanes = lax.broadcasted_iota(jnp.int32, (1, length * BLOCK), 1)
        live = jnp.where(lanes < used * BLOCK, 1.0, 0.0).astype(BF16)
        ones = jnp.broadcast_to(live, (HEAD_DIM, length * BLOCK))
        now = g % 2

        def prepare(r):
            right = picked_ref[r]
            keys_ref[r] = (nn(right, wk_ref[...]) * KEY_SCALE).astype(BF16)
            values_ref[r] = nt(wvt_ref[...], right).astype(BF16) * live
            for h in range(HEADS):
                rows = slice(h * HEAD_DIM, (h + 1) * HEAD_DIM)
                spread_ref[r, rows, h * BLOCK : (h + 1) * BLOCK] = query_ref[
                    now, rows, r * BLOCK : (r + 1) * BLOCK
                ]

        def score(i):
            r, pair = divmod(i, PAIRS)
            top = None
            for k in range(length):
                keys = keys_ref[r, k * BLOCK : (k + 1) * BLOCK]
                part = nn(keys, spread_ref[r, :, pair * 2 * BLOCK : (pair + 1) * 2 * BLOCK])
                scores_ref[i % SLOTS, k * BLOCK : (k + 1) * BLOCK] = part
                tile = jnp.max(part.reshape(BLOCK // 8, 8, 2 * BLOCK), axis=0)
                top = tile if top is None else jnp.maximum(top, tile)
            top_ref[i % SLOTS] = jnp.broadcast_to(
                jnp.max(top, axis=0, keepdims=True), (8, 2 * BLOCK)
            )

        def process(i):
            r, pair = divmod(i, PAIRS)
            weights = shifted_weights(scores_ref[i % SLOTS], top_ref[i % SLOTS])
            rows = slice(pair * 2 * HEAD_DIM, (pair + 1) * 2 * HEAD_DIM)
            mixed = nn(jnp.concatenate([values_ref[r, rows], ones], axis=0), weights)
            inverse = 1.0 / mixed[2 * HEAD_DIM : 2 * HEAD_DIM + 1]
            here = slice(r * BLOCK, (r + 1) * BLOCK)
            start = pair * 2 * HEAD_DIM
            mix_ref[now, start : start + HEAD_DIM, here] = (
                mixed[:HEAD_DIM, :BLOCK] * inverse[:, :BLOCK]
            ).astype(BF16)
            mix_ref[now, start + HEAD_DIM : start + 2 * HEAD_DIM, here] = (
                mixed[HEAD_DIM : 2 * HEAD_DIM, BLOCK:] * inverse[:, BLOCK:]
            ).astype(BF16)

        prepare(0)
        for i in range(AHEAD):
            score(i)
        out_stage(jnp.maximum(g - 1, 0))
        for i in range(STEPS):
            if i % PAIRS == 0 and i // PAIRS + 1 < BAND:
                prepare(i // PAIRS + 1)
            if i + AHEAD < STEPS:
                score(i + AHEAD)
            process(i)
            if i == RELAY_STEP:
                pl.when(g > 0)(lambda: out_copy(g - 1).start())
                branches(g, lambda fixed: relay(fixed + LEAD))
            if i == FORWARD_STEP:
                branches(g, lambda fixed: forward(fixed + 1))
        query_stage(jnp.minimum(g + 1, bands - 1))
        return carry

    lax.fori_loop(0, bands, band_step, 0)
    out_stage(bands - 1)
    out_copy(bands - 1).start()

    for hop in range(len(start_hops)):
        coarse_copy(hop).wait_send()
    for g in range(bands):
        for hop in range(len(fine_hops)):
            fine_copy(g, hop).wait_send()
        out_copy(g).wait()


def finish_kernel(fine_ref, prior_ref, fine_out, prior_out, fine_buf, prior_buf, into, out_of):
    parts = into.shape[0] - 1
    size = fine_ref.shape[0] // parts
    steps = [
        (fine_ref.at[here], fine_buf.at[here], fine_out.at[here])
        for here in (pl.ds(i * size, size) for i in range(parts))
    ]
    steps.append((prior_ref, prior_buf, prior_out))
    loads = [
        pltpu.make_async_copy(source, held, into.at[i]) for i, (source, held, _) in enumerate(steps)
    ]
    stores = [
        pltpu.make_async_copy(held, target, out_of.at[i])
        for i, (_, held, target) in enumerate(steps)
    ]
    for load in loads:
        load.start()
    for load, store in zip(loads, stores):
        load.wait()
        store.start()
    for store in stores:
        store.wait()


def finish(fine, prior):
    hbm = pl.BlockSpec(memory_space=pl.ANY)
    parts = min(PARTS, fine.shape[0])
    return pl.pallas_call(
        finish_kernel,
        out_shape=(
            jax.ShapeDtypeStruct(fine.shape, BF16),
            jax.ShapeDtypeStruct(prior.shape, BF16),
        ),
        in_specs=[hbm, hbm],
        out_specs=(hbm, hbm),
        scratch_shapes=[
            pltpu.VMEM(fine.shape, BF16),
            pltpu.VMEM(prior.shape, BF16),
            pltpu.SemaphoreType.DMA((parts + 1,)),
            pltpu.SemaphoreType.DMA((parts + 1,)),
        ],
        compiler_params=pltpu.CompilerParams(vmem_limit_bytes=60 * 1024 * 1024),
        name="finish",
    )(fine, prior)


def body(
    left_fine,
    right_fine,
    left_coarse,
    right_coarse,
    candidates,
    counts,
    query_weight,
    key_weight,
    value_weight,
    out_weight,
    norm_gain,
):
    n = lax.axis_size("cols")
    rows, cols, feat = left_fine.shape
    bands = rows // BAND
    coarse_rows, coarse_cols, _ = left_coarse.shape
    length = candidates.shape[2]
    up = upsample_matrix(coarse_cols)
    fold = np.tile(np.eye(coarse_cols, dtype=np.float32), (1, HEADS))
    hop_count = len(gather_hops(n, 0))
    many = n * coarse_cols
    wide = HEADS * coarse_cols
    vmem = pl.BlockSpec(memory_space=pltpu.VMEM)
    smem = pl.BlockSpec(memory_space=pltpu.SMEM)
    hbm = pl.BlockSpec(memory_space=pl.ANY)
    out = pl.pallas_call(
        functools.partial(kernel, n=n, row_devices=lax.axis_size("rows"), bands=bands),
        out_shape=(
            jax.ShapeDtypeStruct(left_fine.shape, BF16),
            jax.ShapeDtypeStruct(left_coarse.shape, BF16),
        ),
        in_specs=[smem, smem, hbm, hbm] + [vmem] * 9,
        out_specs=(hbm, vmem),
        scratch_shapes=[pltpu.VMEM((n, BAND, cols, feat), BF16) for _ in range(bands)]
        + [
            pltpu.VMEM(left_fine.shape, BF16),
            pltpu.VMEM(left_fine.shape, BF16),
            pltpu.VMEM((n,) + right_coarse.shape, BF16),
            pltpu.VMEM((coarse_rows + 2, coarse_cols + 2 * EDGE, feat), BF16),
            pltpu.VMEM((feat, feat), BF16),
            pltpu.VMEM((feat, feat), BF16),
            pltpu.VMEM((coarse_rows, many, feat), BF16),
            pltpu.VMEM((coarse_rows, feat, many), BF16),
            pltpu.VMEM((coarse_rows * coarse_cols, feat), BF16),
            pltpu.VMEM((coarse_rows, many, wide), F32),
            pltpu.VMEM((coarse_rows, 8, wide), F32),
            pltpu.VMEM((BAND, length * BLOCK, feat), BF16),
            pltpu.VMEM((2, BAND * BLOCK, feat), BF16),
            pltpu.VMEM((2, feat, BAND * BLOCK), BF16),
            pltpu.VMEM((BAND, length * BLOCK, feat), BF16),
            pltpu.VMEM((BAND, feat, length * BLOCK), BF16),
            pltpu.VMEM((BAND, feat, HEADS * BLOCK), BF16),
            pltpu.VMEM((SLOTS, length * BLOCK, 2 * BLOCK), F32),
            pltpu.VMEM((SLOTS, 8, 2 * BLOCK), F32),
            pltpu.VMEM((2, feat, BAND * BLOCK), BF16),
            pltpu.SemaphoreType.DMA((hop_count,)),
            pltpu.SemaphoreType.DMA((hop_count,)),
            pltpu.SemaphoreType.DMA((8,)),
            pltpu.SemaphoreType.DMA((8,)),
            pltpu.SemaphoreType.DMA((bands, hop_count)),
            pltpu.SemaphoreType.DMA((bands, hop_count)),
            pltpu.SemaphoreType.DMA((bands,)),
            pltpu.SemaphoreType.DMA((1,)),
            pltpu.SemaphoreType.DMA((bands,)),
        ],
        compiler_params=pltpu.CompilerParams(
            collective_id=0, has_side_effects=True, vmem_limit_bytes=60 * 1024 * 1024
        ),
        name="stereo",
    )(
        jnp.transpose(candidates, (0, 2, 1)),
        counts,
        left_fine,
        right_fine,
        left_coarse,
        right_coarse,
        jnp.asarray(up, BF16),
        query_weight,
        key_weight,
        value_weight,
        out_weight,
        norm_gain.reshape(1, -1),
        jnp.asarray(fold, BF16),
    )
    return finish(*out)


def solution(mesh):
    return jax.shard_map(
        body,
        mesh=mesh,
        in_specs=(
            P("rows", "cols", None),
            P("rows", "cols", None),
            P("rows", "cols", None),
            P("rows", "cols", None),
            P(None, "rows", None),
            P(None, "rows"),
            P(),
            P(),
            P(),
            P(),
            P(),
        ),
        out_specs=(P("rows", "cols", None), P("rows", "cols", None)),
        check_vma=False,
    )
```
